512 devices in a mesh: sub: 16 (over z), row: 4 (over y), col: 8 (over x, core).
Axes of the slice: x: 4, y: 4, z: 16, core: 2. Of those that a mesh axis runs over, the one named last changes fastest.
Arguments:
- child_factor: float32 [16, 256, 2048], P('sub', None, 'row'), may hold values from -6 to 6
- child_map: int32 [16, 2048], P('sub'), may hold values from 0 to 8191, as said below
- child_len: int32 [16], P('sub'), may hold values from 1 to 2048, 16384 in all
- class_ids: int32 [8192], replicated, may hold values from 0 to 7
- class_kappa: float32 [8], replicated, may hold values from 0.25 to 16
- landmarks: int32 [256], replicated, may hold values from 0 to 1023
- diag_inverse: float32 [2, 512, 512], replicated, as said below
Outputs:
- panel_factor: float32 [2, 512, 16, 512], P(None, 'col', 'sub', 'row')
- landmark_solution: float32 [256, 16, 512], P('col', 'sub', 'row')
The draws below stay inside these ranges and needn't reach their ends.
Inputs may be any that keep to these rules, and one draw needn't show every extreme that they name: `child_map`: node i of a child maps to parent row 512 a + 128 (i // 512) + u for some block a and some u below 128; the nodes of one child map to distinct rows. `diag_inverse`: each 512 x 512 block is lower triangular with a positive diagonal.
All inputs are finite; a program needn't handle non-finite values. No bound on the sum of `child_len` on one device may be relied on, other than what follows from the above.
Results may differ from the reference program's by a relative error of at most 0.0003.
Values sent between devices are 32-bit elements; how exact they have to be, the bound alone decides.
A program may use at most 64 MiB of HBM per device.

```python
import math
import jax
import jax.numpy as jnp
import numpy as np
from jax import lax

NF = 8192
PW = 512
PANELS = 2
MC = 2048
KCH = 256
NLM = 256
NCLASS = 8
CHILDREN = 16
RB = 16
WINDOW = 1024
QROWS = 128
NODEQ = 512


def draw_child_map(key, part):
    base_key = jax.random.fold_in(key, 11)

    def one_quarter(child_key, quarter_index):
        slot_order = jax.random.permutation(jax.random.fold_in(child_key, quarter_index), RB * QROWS)[:NODEQ]
        return slot_order // QROWS * PW + quarter_index * QROWS + slot_order % QROWS

    def one_child(child_index):
        child_key = jax.random.fold_in(base_key, child_index)
        return jnp.concatenate([one_quarter(child_key, quarter_index) for quarter_index in range(MC // NODEQ)]).astype(jnp.int32)
    return jnp.stack([one_child(child_index) for child_index in range(CHILDREN)])


def draw_diag_inverse(key, part):
    noise_key, scale_key = jax.random.split(jax.random.fold_in(key, 23))
    row_index = jnp.arange(PW, dtype=jnp.int32)[:, None]
    col_index = jnp.arange(PW, dtype=jnp.int32)[None, :]
    lower_mask = (col_index < row_index).astype(jnp.float32)
    diag_mask = (col_index == row_index).astype(jnp.float32)
    spread = jax.random.normal(noise_key, (PANELS, PW, PW), jnp.float32) * 0.0006
    diag_scale = jnp.exp(jax.random.uniform(scale_key, (PANELS, PW, 1), jnp.float32, jnp.log(0.005), jnp.log(0.015)))
    return spread * lower_mask + diag_scale * diag_mask


def plant(entries, stream_key, least, high):
    extent = entries.shape
    index_at = [jax.random.randint(jax.random.fold_in(stream_key, axis), (), 0, extent[axis]) for axis in range(len(extent))]
    entries = entries.at[tuple(index_at)].set(least)
    longest = extent.index(max(extent))
    index_at[longest] = (index_at[longest] + 1) % extent[longest]
    return entries.at[tuple(index_at)].set(high)


def steps_of(own_key, dims, shards, least, high):
    loudness, own = 1.0, jax.random.fold_in(own_key, 6)
    for axis_at, parts in shards:
        heights = jnp.exp(jax.random.uniform(jax.random.fold_in(own, axis_at), (parts,), jnp.float32, least / len(shards), high / len(shards)))
        loudness = loudness * jnp.repeat(heights, dims[axis_at] // parts).reshape([-1 if axis == axis_at else 1 for axis in range(len(dims))])
    return loudness


def length_profile(number_of, total, bound, skew):
    loads = [(1 << 20) // math.isqrt(grade ** skew) + 1 for grade in range(2, number_of + 1)]
    surplus, holding = total - bound - (number_of - 1), [1] * (number_of - 1)
    while surplus > 0:
        candidates = [i for i in range(number_of - 1) if holding[i] < bound]
        mass, left = sum([loads[i] for i in candidates]), surplus
        for i in candidates:
            more = min(bound - holding[i], max(1, left * loads[i] // mass), surplus)
            holding[i] = holding[i] + more
            surplus = surplus - more
    return np.array([bound] + holding)


def uneven_parts(stream_key, amount, total, bound, lean):
    if amount == 2:
        one = jax.random.randint(stream_key, (), max(1, total - bound), min(bound, total - 1) + 1)
        return jnp.stack([one, total - one])
    tallies = jnp.asarray(length_profile(amount, total, bound, lean), jnp.int32)
    pairs = (amount - 1) // 2
    donor, taker = tallies[1:1 + 2 * pairs:2], tallies[2:2 + 2 * pairs:2]
    room = jnp.minimum(donor - 1, bound - taker)
    moved = jax.random.randint(jax.random.fold_in(stream_key, 1), (pairs,), 0, 1 << 20) % (room + 1)
    tallies = tallies.at[1:1 + 2 * pairs:2].set(donor - moved).at[2:2 + 2 * pairs:2].set(taker + moved)
    return tallies[jax.random.permutation(jax.random.fold_in(stream_key, 2), amount)]


def gaussian(own_key, dims, scale, bound, cuts=(), kind=jnp.bfloat16):
    loudness = steps_of(own_key, dims, cuts, -0.22, 0.18) if cuts else 1.0
    result = jax.random.normal(own_key, dims, jnp.float32) * scale * loudness
    return jnp.minimum(jnp.maximum(result, -bound), bound).astype(kind)


def setup_inputs(seed: int = 0) -> dict:
    splits = jax.random.split(jax.random.key(seed), 8)
    child_factor = gaussian(splits[0], (CHILDREN, KCH, MC), (8.4 * KCH ** -0.25), 6.0, ((0, 16), (2, 4)), jnp.float32)
    child_map = draw_child_map(jax.random.fold_in(splits[7], 71), 0)
    child_len = uneven_parts(splits[2], CHILDREN, CHILDREN * MC // 2, MC, 2).astype(jnp.int32)
    class_ids = plant(jax.random.randint(splits[3], (NF,), 0, NCLASS), jax.random.fold_in(splits[3], 1), 0, NCLASS - 1).astype(jnp.int32)
    class_kappa = jnp.clip(jnp.exp(jax.random.uniform(splits[4], (NCLASS,), jnp.float32, math.log(0.25), math.log(16.0))), 0.25, 16.0)
    landmarks = plant(jax.random.randint(splits[5], (NLM,), 0, WINDOW), jax.random.fold_in(splits[5], 1), 0, WINDOW - 1).astype(jnp.int32)
    diag_inverse = draw_diag_inverse(jax.random.fold_in(splits[7], 71), 0)
    return {"child_factor": child_factor, "child_map": child_map, "child_len": child_len, "class_ids": class_ids, "class_kappa": class_kappa, "landmarks": landmarks, "diag_inverse": diag_inverse}


PRECISE = lax.Precision.HIGHEST


def reference(child_factor, child_map, child_len, class_ids, class_kappa, landmarks, diag_inverse):
    node_index = jnp.arange(MC, dtype=jnp.int32)
    columns = jnp.arange(WINDOW, dtype=jnp.int32)

    def add_child(front_acc, inputs):
        factor, node_map, length = inputs
        live_factor = jnp.where((node_index < length)[None, :], factor, jnp.float32(0.0))
        select = (node_map[:, None] == columns[None, :]).astype(jnp.float32)
        reduced = jnp.dot(live_factor, select, precision=PRECISE)
        update = -jnp.dot(live_factor.T, reduced, precision=PRECISE)
        return front_acc.at[node_map].add(update), None

    front_acc, _ = lax.scan(add_child, jnp.zeros((NF, WINDOW), jnp.float32), (child_factor, child_map, child_len))
    coefficient = class_kappa[class_ids] + jnp.float32(4.0)
    row_index = jnp.arange(NF, dtype=jnp.int32)
    offset_band = row_index[:, None] - columns[None, :]
    end_count = jnp.where((row_index == 0) | (row_index == NF - 1), jnp.float32(1.0), jnp.float32(2.0))
    coeff_row = coefficient[:, None]
    coeff_col = coefficient[:WINDOW][None, :]
    band_part = jnp.where(offset_band == 0, coeff_row * coeff_row + end_count[:, None],
                          jnp.where(jnp.abs(offset_band) == 1, -(coeff_row + coeff_col),
                                    jnp.where(jnp.abs(offset_band) == 2, jnp.float32(1.0), jnp.float32(0.0))))
    front_acc = front_acc + band_part
    right_side = front_acc[:, landmarks]
    factor_all = jnp.zeros((NF, WINDOW), jnp.float32)
    inner_index = jnp.arange(PW, dtype=jnp.int32)
    block_index = row_index // PW
    for panel_index in range(PANELS):
        first_col = panel_index * PW
        panel_now = jnp.dot(front_acc[:, first_col:first_col + PW], diag_inverse[panel_index].T, precision=PRECISE)
        keep_mask = (row_index[:, None] - first_col) >= inner_index[None, :]
        panel_now = jnp.where(keep_mask, panel_now, jnp.float32(0.0))
        factor_all = factor_all.at[:, first_col:first_col + PW].set(panel_now)
        for later_panel in range(panel_index + 1, PANELS):
            later_first = later_panel * PW
            front_acc = front_acc.at[:, later_first:later_first + PW].add(
                -jnp.dot(panel_now, panel_now[later_first:later_first + PW].T, precision=PRECISE))
        values = jnp.dot(diag_inverse[panel_index], right_side[first_col:first_col + PW], precision=PRECISE)
        below_update = jnp.dot(panel_now, values, precision=PRECISE)
        right_side = jnp.where((block_index > panel_index)[:, None], right_side - below_update, right_side)
        right_side = right_side.at[first_col:first_col + PW].set(values)
    panel_factor = factor_all.reshape(RB, PW, PANELS, PW).transpose(2, 3, 0, 1)
    landmark_solution = right_side.T.reshape(NLM, RB, PW)
    return panel_factor, landmark_solution
```

```python
import jax
import jax.numpy as jnp
from jax import lax
from jax.experimental import pallas as pl
from jax.experimental.pallas import tpu as pltpu
from jax.sharding import PartitionSpec as P

F32 = jnp.float32
BF16 = jnp.bfloat16
MESH = pl.DeviceIdType.MESH

NSUB, NROW, NCOL = 16, 4, 8
PW, Q, CW, KCH, NODEQ, NLAND = 512, 128, 64, 256, 512, 32
CHUNKS = 2
CROWS = 2 * CW // CHUNKS


def dg(a, b, ca, cb):
    return lax.dot_general(a, b, (((ca,), (cb,)), ((), ())), preferred_element_type=F32)


def split(x):
    hi = x.astype(BF16)
    return hi, (x - hi.astype(F32)).astype(BF16)


def mm(a, b_hi, b_lo, cb):
    n = a.shape[0]
    a_hi, a_lo = split(a)
    both = dg(jnp.concatenate([a_hi, a_lo], axis=0), b_hi, 1, cb)
    return both[:n] + both[n:] + dg(a_hi, b_lo, 1, cb)


def lanes(shape):
    return lax.broadcasted_iota(jnp.int32, shape, 1)


def rows_of(shape):
    return lax.broadcasted_iota(jnp.int32, shape, 0)


def kernel(
    factor_hbm, map_ref, len_ref, ids_ref, kappa_ref, land_ref, dinv_hbm,
    pf_ref, ls_ref,
    factor, dinv, live_hi, live_lo, red_out, red_in, redl, pst,
    top_out, top_in, top_own, top_all, front_top, rland, s_hi, s_lo,
    first, ring_p, ring_m, fx,
    ld_sem, red_s, red_r, redl_s, redl_r, top_s, top_r, tag_s, tag_r,
    pla_s, pla_r, fwd_s, fwd_r, rl_s, rl_r,
    rp_s, rp_r, rm_s, rm_r, xa_s, xa_r, xf_s, xf_r,
):
    s = lax.axis_index("sub")
    r = lax.axis_index("row")
    c = lax.axis_index("col")
    x, h = c // 2, c % 2
    other = {"col": 2 * x + 1 - h}
    group = 2 * ((r + x) % NROW) + h

    load_factor = pltpu.make_async_copy(factor_hbm.at[0], factor, ld_sem.at[0])
    load_factor.start()
    load_dinv = pltpu.make_async_copy(dinv_hbm, dinv, ld_sem.at[1])
    load_dinv.start()
    barrier = pltpu.get_barrier_semaphore()

    def greet_z(k, carry):
        pl.semaphore_signal(barrier, inc=1, device_id={"sub": (s + k) % NSUB}, device_id_type=MESH)
        return carry

    def plane_peer(k):
        m = (r * 4 + x + k) % 16
        return m // 4, m % 4

    def greet_plane(k, carry):
        pr, px = plane_peer(k)
        pl.semaphore_signal(barrier, inc=1, device_id={"row": pr, "col": 2 * px + h}, device_id_type=MESH)
        return carry

    lax.fori_loop(1, NSUB, greet_z, 0)
    lax.fori_loop(1, 16, greet_plane, 0)
    pl.semaphore_signal(barrier, inc=1, device_id=other, device_id_type=MESH)

    node_row = map_ref[:, pl.ds(pl.multiple_of(r * NODEQ, NODEQ), NODEQ)]
    land_row = land_ref[...]
    land_col = jnp.sum(
        jnp.where(lanes((NLAND, 256)) == rows_of((NLAND, 256)) + c * NLAND, land_row.astype(F32), 0.0),
        axis=1, keepdims=True,
    ).astype(jnp.int32)
    iota_col = rows_of((2 * CW, 1))
    send_cols = iota_col // CW * PW + (2 * r + h) * CW + iota_col % CW
    own_cols = iota_col // CW * PW + group * CW + iota_col % CW
    select = jnp.concatenate([send_cols, land_col], axis=0) == node_row
    select = jnp.where(select, 1.0, 0.0).astype(BF16)
    load_factor.wait()
    live = jnp.where(lanes((KCH, NODEQ)) + r * NODEQ < len_ref[0], factor[...], 0.0)
    lh, ll = split(live)
    live_hi[...] = lh
    live_lo[...] = ll
    reduced = dg(select, lh, 1, 1) + dg(select, ll, 1, 1)
    red_out[...] = reduced[: 2 * CW]
    redl[r] = reduced[2 * CW :]

    pl.semaphore_wait(barrier, 31)

    red_copy = pltpu.make_async_remote_copy(
        src_ref=red_out, dst_ref=red_in, send_sem=red_s.at[0], recv_sem=red_r.at[0],
        device_id={"row": (r - x + NROW) % NROW}, device_id_type=MESH,
    )

    @pl.when(x != 0)
    def _():
        red_copy.start()

    @pl.when(x == 0)
    def _():
        red_in[...] = red_out[...]

    def redl_copy(src_row, dst_row):
        return pltpu.make_async_remote_copy(
            src_ref=redl.at[src_row], dst_ref=redl.at[src_row],
            send_sem=redl_s.at[dst_row], recv_sem=redl_r.at[src_row],
            device_id={"row": dst_row}, device_id_type=MESH,
        )

    for k in range(1, NROW):
        redl_copy(r, (r + k) % NROW).start()

    def band(columns, block):
        index = block * NROW + r
        near = jnp.concatenate(
            [
                ids_ref[pl.ds(jnp.maximum(index - 1, 0), 1), :],
                ids_ref[pl.ds(index, 1), :],
                ids_ref[pl.ds(jnp.minimum(index + 1, 63), 1), :],
            ],
            axis=1,
        )
        coef = jnp.zeros(near.shape, F32)
        for k in range(8):
            coef = jnp.where(near == k, kappa_ref[k], coef)
        coef = coef + 4.0
        here = coef[:, Q : 2 * Q]
        before = pltpu.roll(coef, 1, 1)[:, Q : 2 * Q]
        after = pltpu.roll(coef, 3 * Q - 1, 1)[:, Q : 2 * Q]
        row = index * Q + lanes((1, Q))
        ends = jnp.where((row == 0) | (row == 64 * Q - 1), 1.0, 2.0)
        off = row - columns
        return jnp.where(
            off == 0, here * here + ends,
            jnp.where(
                off == 1, -(here + before),
                jnp.where(off == -1, -(here + after), jnp.where(jnp.abs(off) == 2, 1.0, 0.0)),
            ),
        )

    target = node_row // PW * Q + node_row % Q
    top_band = jnp.concatenate(
        [band(own_cols[:CW], 1), band(land_col, 0), band(land_col, 1)], axis=0
    )
    top_band = jnp.where(s == 0, top_band, 0.0)
    own_band = band(own_cols, s)

    @pl.when(x != 0)
    def _():
        red_copy.wait_recv()

    for k in range(1, NROW):
        redl_copy((r + k) % NROW, r).wait_recv()
    reduced_all = jnp.concatenate([red_in[...], redl[0] + redl[1] + redl[2] + redl[3]], axis=0)
    part = -mm(reduced_all, live_hi[...], live_lo[...], 0)
    part_hi, part_lo = split(part)
    pst[...] = jnp.concatenate([part_hi[: 2 * CW], part_lo[: 2 * CW]], axis=0)

    place_top = jnp.where(target == rows_of((2 * Q, 1)), 1.0, 0.0).astype(BF16)
    top = dg(jnp.concatenate([part_hi, part_lo], axis=0), place_top, 1, 1)
    top = top[: 2 * CW + NLAND] + top[2 * CW + NLAND :]
    top_out[...] = top_band + jnp.concatenate(
        [top[:CW, Q:], top[2 * CW :, :Q], top[2 * CW :, Q:]], axis=0
    )

    def top_copy(src_sub, dst_sub):
        return pltpu.make_async_remote_copy(
            src_ref=top_out.at[pl.ds(pl.multiple_of(dst_sub * 8, 8), 8)], dst_ref=top_in.at[src_sub],
            send_sem=top_s.at[dst_sub], recv_sem=top_r.at[src_sub],
            device_id={"sub": dst_sub}, device_id_type=MESH,
        )

    def top_start(k, carry):
        top_copy(s, (s + k) % NSUB).start()
        return carry

    lax.fori_loop(1, NSUB, top_start, 0)

    right = {"sub": (s + 1) % NSUB}
    left = {"sub": (s + NSUB - 1) % NSUB}

    def contribution(block_a, block_b):
        place = rows_of((2 * Q, 1))
        place = jnp.where(place < Q, block_a * Q + place, block_b * Q + place - Q)
        place = jnp.where(target == place, 1.0, 0.0).astype(BF16)
        both = dg(pst[...], place, 1, 1)
        both = both[: 2 * CW] + both[2 * CW :]
        return both[:, :Q], both[:, Q:]

    def ring_copy(src, ring, send, recv, step, chunk, where):
        part_of = pl.ds(chunk * CROWS, CROWS)
        return pltpu.make_async_remote_copy(
            src_ref=src.at[part_of], dst_ref=ring.at[step, part_of],
            send_sem=send.at[step, chunk], recv_sem=recv.at[step, chunk],
            device_id=where, device_id_type=MESH,
        )

    def copy_p(src, step, chunk):
        return ring_copy(src, ring_p, rp_s, rp_r, step, chunk, right)

    def copy_m(src, step, chunk):
        return ring_copy(src, ring_m, rm_s, rm_r, step, chunk, left)

    to_right, to_left = contribution((s + 8) % NSUB, (s + 9) % NSUB)
    first[0] = to_right
    first[1] = to_left
    for chunk in range(CHUNKS):
        copy_p(first.at[0], 0, chunk).start()
        copy_m(first.at[1], 0, chunk).start()

    def ring_step(t, carry):
        to_right, to_left = contribution((s + 8 - t) % NSUB, (s + 9 + t) % NSUB)
        for chunk in range(CHUNKS):
            part_of = pl.ds(chunk * CROWS, CROWS)
            static = slice(chunk * CROWS, (chunk + 1) * CROWS)
            copy_p(ring_p.at[t - 1], t - 1, chunk).wait_recv()
            ring_p[t - 1, part_of, :] += to_right[static]
            copy_p(ring_p.at[t - 1], t, chunk).start()
            copy_m(ring_m.at[t - 1], t - 1, chunk).wait_recv()
            ring_m[t - 1, part_of, :] += to_left[static]
            copy_m(ring_m.at[t - 1], t, chunk).start()
        return carry

    def top_wait(k, carry):
        top_copy((s + k) % NSUB, s).wait_recv()
        return carry

    lax.fori_loop(1, NSUB, top_wait, 0)
    top_in[s] = top_out[pl.ds(pl.multiple_of(s * 8, 8), 8), :]
    top_own[...] = jnp.sum(top_in[...], axis=0)

    def tag_copy(src_sub, dst_sub):
        return pltpu.make_async_remote_copy(
            src_ref=top_own, dst_ref=top_all.at[pl.ds(pl.multiple_of(src_sub * 8, 8), 8)],
            send_sem=tag_s.at[dst_sub], recv_sem=tag_r.at[src_sub],
            device_id={"sub": dst_sub}, device_id_type=MESH,
        )

    def tag_start(k, carry):
        tag_copy(s, (s + k) % NSUB).start()
        return carry

    lax.fori_loop(1, NSUB, tag_start, 0)
    top_all[pl.ds(pl.multiple_of(s * 8, 8), 8), :] = top_own[...]

    lax.fori_loop(1, 3, ring_step, 0)

    def tag_wait(k, carry):
        tag_copy((s + k) % NSUB, s).wait_recv()
        return carry

    lax.fori_loop(1, NSUB, tag_wait, 0)

    def piece(pr, px, ph):
        g = 2 * ((pr + px) % NROW) + ph
        return front_top.at[pr, pl.ds(pl.multiple_of(g * CW, CW), CW)]

    def plane_copy(src_row, src_x, dst_row, dst_x):
        return pltpu.make_async_remote_copy(
            src_ref=top_all.at[pl.ds(0, CW)], dst_ref=piece(src_row, src_x, h),
            send_sem=pla_s.at[dst_row * 4 + dst_x], recv_sem=pla_r.at[src_row * 4 + src_x],
            device_id={"row": dst_row, "col": 2 * dst_x + h}, device_id_type=MESH,
        )

    def fwd_copy(pr, px, src, ph):
        return pltpu.make_async_remote_copy(
            src_ref=src, dst_ref=piece(pr, px, ph),
            send_sem=fwd_s.at[pr * 4 + px], recv_sem=fwd_r.at[pr * 4 + px],
            device_id=other, device_id_type=MESH,
        )

    def rland_copy(src_row, dst_row):
        return pltpu.make_async_remote_copy(
            src_ref=top_all.at[pl.ds(CW, 2 * NLAND)], dst_ref=rland.at[src_row],
            send_sem=rl_s.at[dst_row], recv_sem=rl_r.at[src_row],
            device_id={"row": dst_row}, device_id_type=MESH,
        )

    def plane_start(k, carry):
        pr, px = plane_peer(k)
        plane_copy(r, x, pr, px).start()
        return carry

    lax.fori_loop(1, 16, plane_start, 0)
    for k in range(1, NROW):
        rland_copy(r, (r + k) % NROW).start()
    fwd_copy(r, x, top_all.at[pl.ds(0, CW)], h).start()
    front_top[r, pl.ds(pl.multiple_of(group * CW, CW), CW), :] = top_all[:CW]
    rland[r] = top_all[CW:]

    lax.fori_loop(3, 6, ring_step, 0)

    load_dinv.wait()
    for k in range(2):
        d_hi, d_lo = split(dinv[k])
        gram = dg(d_hi, d_hi, 0, 0) + dg(d_hi, d_lo, 0, 0) + dg(d_lo, d_hi, 0, 0)
        g_hi, g_lo = split(gram)
        s_hi[k] = g_hi
        s_lo[k] = g_lo

    def plane_forward(k, carry):
        pr, px = plane_peer(16 - k)
        plane_copy(pr, px, r, x).wait_recv()
        fwd_copy(pr, px, piece(pr, px, h), h).start()
        return carry

    lax.fori_loop(1, 16, plane_forward, 0)
    lax.fori_loop(6, 7, ring_step, 0)

    to_right, own = contribution((s + 1) % NSUB, s)
    for chunk in range(CHUNKS):
        part_of = pl.ds(chunk * CROWS, CROWS)
        static = slice(chunk * CROWS, (chunk + 1) * CROWS)
        copy_p(ring_p.at[6], 6, chunk).wait_recv()
        ring_p[6, part_of, :] += to_right[static]
        copy_p(ring_p.at[6], 7, chunk).start()
    own = own + own_band
    for chunk in range(CHUNKS):
        part_of = pl.ds(chunk * CROWS, CROWS)
        static = slice(chunk * CROWS, (chunk + 1) * CROWS)
        copy_m(ring_m.at[6], 6, chunk).wait_recv()
        copy_p(ring_p.at[7], 7, chunk).wait_recv()
        fx[group, part_of, :] = own[static] + ring_m[6, part_of, :] + ring_p[7, part_of, :]

    def slot(px, ph):
        return 2 * ((r + px) % NROW) + ph

    def xag_copy(src_x, dst_x):
        return pltpu.make_async_remote_copy(
            src_ref=fx.at[slot(src_x, h)], dst_ref=fx.at[slot(src_x, h)],
            send_sem=xa_s.at[dst_x], recv_sem=xa_r.at[src_x],
            device_id={"col": 2 * dst_x + h}, device_id_type=MESH,
        )

    def xfwd_copy(px, ph):
        return pltpu.make_async_remote_copy(
            src_ref=fx.at[slot(px, ph)], dst_ref=fx.at[slot(px, ph)],
            send_sem=xf_s.at[px], recv_sem=xf_r.at[px],
            device_id=other, device_id_type=MESH,
        )

    for k in range(1, 4):
        xag_copy(x, (x + k) % 4).start()
    xfwd_copy(x, h).start()

    def fwd_wait(k, carry):
        pr, px = k // 4, k % 4
        fwd_copy(pr, px, piece(pr, px, 1 - h), 1 - h).wait_recv()
        return carry

    lax.fori_loop(0, 16, fwd_wait, 0)
    for k in range(1, NROW):
        rland_copy((r + k) % NROW, r).wait_recv()
    f_hi, f_lo = split(jnp.concatenate([front_top[k] for k in range(NROW)], axis=1))
    r0 = jnp.concatenate([rland[k, :NLAND] for k in range(NROW)], axis=1)
    r1 = jnp.concatenate([rland[k, NLAND:] for k in range(NROW)], axis=1)
    own_rows = pl.ds(pl.multiple_of(c * CW, CW), CW)
    d0_own = dinv[0, own_rows, :]
    d1_own = dinv[1, own_rows, :]
    w0 = mm(r0, s_hi[0], s_lo[0], 0)
    t1 = r1 - mm(w0, f_hi, f_lo, 0)
    w1 = mm(t1, s_hi[1], s_lo[1], 0)
    back = mm(jnp.concatenate([d1_own, w1], axis=0), f_hi, f_lo, 1)
    back = mm(back, s_hi[0], s_lo[0], 0)
    column = lanes((NLAND, PW))
    e0 = jnp.where(column == land_col, 1.0, 0.0)
    e1 = jnp.where(column + PW == land_col, 1.0, 0.0)
    left0 = jnp.concatenate([d0_own, -back[:CW], e0 - w0 + back[CW:]], axis=0)
    left1 = jnp.concatenate([d1_own, e1 - w1], axis=0)

    for k in range(1, 4):
        px = (x + k) % 4
        xag_copy(px, x).wait_recv()
        xfwd_copy(px, h).start()
    for k in range(4):
        xfwd_copy(k, 1 - h).wait_recv()
    f0_hi, f0_lo = split(jnp.concatenate([fx[k, :CW] for k in range(NCOL)], axis=0))
    f1_hi, f1_lo = split(jnp.concatenate([fx[k, CW:] for k in range(NCOL)], axis=0))
    out0 = mm(left0, f0_hi, f0_lo, 0)
    out1 = mm(left1, f1_hi, f1_lo, 0)
    row_in = s * PW + r * Q + lanes((CW, Q))
    col_in = c * CW + rows_of((CW, Q))
    pf_ref[:CW] = jnp.where(row_in >= col_in, out0[:CW], 0.0)
    pf_ref[CW:] = jnp.where(row_in - PW >= col_in, out0[CW : 2 * CW] + out1[:CW], 0.0)
    ls_ref[...] = out0[2 * CW :] + out1[CW:]

    own_quarter = pl.ds(pl.multiple_of(r * Q, Q), Q)

    @pl.when(s == 0)
    def _():
        d_hi, d_lo = split(dinv[0, own_quarter, :])
        ls_ref[...] = mm(r0, d_hi, d_lo, 1)

    @pl.when(s == 1)
    def _():
        d_hi, d_lo = split(dinv[1, own_quarter, :])
        ls_ref[...] = mm(t1, d_hi, d_lo, 1)

    @pl.when(x != 0)
    def _():
        red_copy.wait_send()

    for k in range(1, NROW):
        redl_copy(r, (r + k) % NROW).wait_send()
        rland_copy(r, (r + k) % NROW).wait_send()
        xag_copy(x, (x + k) % 4).wait_send()

    def sent_z(k, carry):
        top_copy(s, (s + k) % NSUB).wait_send()
        tag_copy(s, (s + k) % NSUB).wait_send()
        return carry

    lax.fori_loop(1, NSUB, sent_z, 0)

    def sent_plane(k, carry):
        pr, px = plane_peer(k)
        plane_copy(r, x, pr, px).wait_send()
        return carry

    lax.fori_loop(1, 16, sent_plane, 0)

    def sent_fwd(k, carry):
        pr, px = k // 4, k % 4
        fwd_copy(pr, px, piece(pr, px, h), h).wait_send()
        return carry

    lax.fori_loop(0, 16, sent_fwd, 0)
    for k in range(4):
        xfwd_copy(k, h).wait_send()
    for chunk in range(CHUNKS):
        copy_p(first.at[0], 0, chunk).wait_send()
        copy_m(first.at[1], 0, chunk).wait_send()

        def sent_ring(t, carry):
            copy_p(ring_p.at[t - 1], t, chunk).wait_send()
            copy_m(ring_m.at[t - 1], t, chunk).wait_send()
            return carry

        lax.fori_loop(1, 7, sent_ring, 0)
        copy_p(ring_p.at[6], 7, chunk).wait_send()


def on_device(child_factor, child_map, child_len, class_ids, class_kappa, landmarks, diag_inverse):
    vmem = pl.BlockSpec(memory_space=pltpu.VMEM)
    smem = pl.BlockSpec(memory_space=pltpu.SMEM)
    hbm = pl.BlockSpec(memory_space=pl.ANY)
    dma = pltpu.SemaphoreType.DMA
    tile = (2 * CW, Q)
    panel_factor, landmark_solution = pl.pallas_call(
        kernel,
        out_shape=(
            jax.ShapeDtypeStruct((2 * CW, Q), F32),
            jax.ShapeDtypeStruct((NLAND, Q), F32),
        ),
        in_specs=[hbm, vmem, smem, vmem, smem, vmem, hbm],
        out_specs=(vmem, vmem),
        scratch_shapes=[
            pltpu.VMEM((KCH, NODEQ), F32),
            pltpu.VMEM((2, PW, PW), F32),
            pltpu.VMEM((KCH, NODEQ), BF16),
            pltpu.VMEM((KCH, NODEQ), BF16),
            pltpu.VMEM((2 * CW, KCH), F32),
            pltpu.VMEM((2 * CW, KCH), F32),
            pltpu.VMEM((NROW, NLAND, KCH), F32),
            pltpu.VMEM((4 * CW, NODEQ), BF16),
            pltpu.VMEM(tile, F32),
            pltpu.VMEM((NSUB, 8, Q), F32),
            pltpu.VMEM((8, Q), F32),
            pltpu.VMEM(tile, F32),
            pltpu.VMEM((NROW, PW, Q), F32),
            pltpu.VMEM((NROW, 2 * NLAND, Q), F32),
            pltpu.VMEM((2, PW, PW), BF16),
            pltpu.VMEM((2, PW, PW), BF16),
            pltpu.VMEM((2,) + tile, F32),
            pltpu.VMEM((8,) + tile, F32),
            pltpu.VMEM((7,) + tile, F32),
            pltpu.VMEM((NCOL,) + tile, F32),
            dma((2,)), dma((1,)), dma((1,)), dma((NROW,)), dma((NROW,)),
            dma((NSUB,)), dma((NSUB,)), dma((NSUB,)), dma((NSUB,)),
            dma((16,)), dma((16,)), dma((16,)), dma((16,)), dma((NROW,)), dma((NROW,)),
            dma((8, CHUNKS)), dma((8, CHUNKS)), dma((8, CHUNKS)), dma((8, CHUNKS)),
            dma((4,)), dma((4,)), dma((4,)), dma((4,)),
        ],
        compiler_params=pltpu.CompilerParams(
            collective_id=0, has_side_effects=True, vmem_limit_bytes=48 << 20
        ),
    )(
        child_factor, child_map, child_len, class_ids.reshape(64, Q), class_kappa,
        landmarks.reshape(1, 256), diag_inverse,
    )
    return panel_factor.reshape(2, CW, 1, Q), landmark_solution.reshape(NLAND, 1, Q)


def solution(mesh):
    return jax.shard_map(
        on_device,
        mesh=mesh,
        in_specs=(P("sub", None, "row"), P("sub", None), P("sub"), P(), P(), P(), P()),
        out_specs=(P(None, "col", "sub", "row"), P("col", "sub", "row")),
        check_vma=False,
    )
```

```python
import jax
import jax.numpy as jnp
from jax import lax
from jax.experimental import pallas as pl
from jax.experimental.pallas import tpu as pltpu
from jax.sharding import PartitionSpec as P

F32 = jnp.float32
BF16 = jnp.bfloat16
MESH = pl.DeviceIdType.MESH

NSUB, NROW, NCOL = 16, 4, 8
NEAR = 4
PW, Q, CW, KCH, NODEQ, NLAND = 512, 128, 64, 256, 512, 32
CHUNKS = 2
CROWS = 2 * CW // CHUNKS


def dg(a, b, ca, cb):
    return lax.dot_general(a, b, (((ca,), (cb,)), ((), ())), preferred_element_type=F32)


def split(x):
    hi = x.astype(BF16)
    return hi, (x - hi.astype(F32)).astype(BF16)


def mm(a, b_hi, b_lo, cb):
    n = a.shape[0]
    a_hi, a_lo = split(a)
    both = dg(jnp.concatenate([a_hi, a_lo], axis=0), b_hi, 1, cb)
    return both[:n] + both[n:] + dg(a_hi, b_lo, 1, cb)


def mod(a, n):
    return lax.rem(a, jnp.int32(n))


def lanes(shape):
    return lax.broadcasted_iota(jnp.int32, shape, 1)


def rows_of(shape):
    return lax.broadcasted_iota(jnp.int32, shape, 0)


def kernel(
    factor_hbm, map_hbm, len_hbm, ids_hbm, kappa_hbm, land_hbm, dinv_hbm,
    pf_ref, ls_ref,
    map_ref, len_ref, ids_ref, kappa_ref, land_ref, factor, dinv, live_hi, live_lo, red_out, red_in, redl, pst,
    top_out, near_in, near_sum, far_in, near_all, top_all, front_top, rland, s_hi, s_lo,
    first, ring_p, ring_m, fx,
    ld_sem, red_s, red_r, redl_s, redl_r, near_s, near_r, far_s, far_r, all_s, all_r,
    fy_s, fy_r, fx_s, fx_r, fwd_s, fwd_r, rl_s, rl_r,
    rp_s, rp_r, rm_s, rm_r, xa_s, xa_r, xf_s, xf_r,
):
    s = lax.axis_index("sub")
    r = lax.axis_index("row")
    c = lax.axis_index("col")
    x, h = lax.div(c, 2), mod(c, 2)
    far, near = lax.div(s, NEAR), mod(s, NEAR)
    other = {"col": 2 * x + 1 - h}
    group = 2 * mod(r + x, NROW) + h
    right = {"sub": mod(s + 1, NSUB)}
    left = {"sub": mod(s + NSUB - 1, NSUB)}

    def near_id(k):
        return {"sub": far * NEAR + mod(near + k, NEAR)}

    def far_id(k):
        return {"sub": mod(s + k * NEAR, NSUB)}

    def row_id(k):
        return {"row": mod(r + k, NROW)}

    def x_id(k):
        return {"col": 2 * mod(x + k, 4) + h}

    def remote(src, dst, send, recv, where):
        return pltpu.make_async_remote_copy(
            src_ref=src, dst_ref=dst, send_sem=send, recv_sem=recv, device_id=where, device_id_type=MESH
        )

    three = pl.ds(0, 3)
    of_redl, of_near, of_far = redl.at[three], near_in.at[three], far_in.at[three]
    of_all, of_row, of_rland = top_all.at[pl.ds(0, 3 * 2 * CW // NEAR)], front_top.at[0, 0, three], rland.at[three]

    def arrived(bytes_of, sem):
        remote(bytes_of, bytes_of, sem, sem, other).wait_recv()

    def departed(bytes_of, sem):
        remote(bytes_of, bytes_of, sem, sem, other).wait_send()

    load_factor = pltpu.make_async_copy(factor_hbm.at[0], factor, ld_sem.at[0])
    load_factor.start()
    small = [
        pltpu.make_async_copy(src, dst, ld_sem.at[2 + k])
        for k, (src, dst) in enumerate(
            [(map_hbm, map_ref), (land_hbm, land_ref), (len_hbm, len_ref), (ids_hbm, ids_ref), (kappa_hbm, kappa_ref)]
        )
    ]
    for copy in small:
        copy.start()
    load_dinv = pltpu.make_async_copy(dinv_hbm, dinv, ld_sem.at[1])
    load_dinv.start()
    barrier = pltpu.get_barrier_semaphore()

    for peer in [right, left, other] + [make(k) for make in (near_id, far_id, row_id, x_id) for k in (1, 2, 3)]:
        pl.semaphore_signal(barrier, inc=1, device_id=peer, device_id_type=MESH)

    for copy in small:
        copy.wait()
    node_row = map_ref[:, pl.ds(pl.multiple_of(r * NODEQ, NODEQ), NODEQ)]
    land_row = land_ref[...]
    land_col = jnp.sum(
        jnp.where(lanes((NLAND, 256)) == rows_of((NLAND, 256)) + c * NLAND, land_row.astype(F32), 0.0),
        axis=1, keepdims=True,
    ).astype(jnp.int32)
    iota_col = rows_of((2 * CW, 1))
    send_cols = iota_col // CW * PW + (2 * r + h) * CW + iota_col % CW
    own_cols = iota_col // CW * PW + group * CW + iota_col % CW
    select = jnp.concatenate([send_cols, land_col], axis=0) == node_row
    select = jnp.where(select, 1.0, 0.0).astype(BF16)
    load_factor.wait()
    live = jnp.where(lanes((KCH, NODEQ)) + r * NODEQ < len_ref[0], factor[...], 0.0)
    lh, ll = split(live)
    live_hi[...] = lh
    live_lo[...] = ll
    reduced = dg(select, lh, 1, 1) + dg(select, ll, 1, 1)
    red_out[...] = reduced[: 2 * CW]
    redl[r] = reduced[2 * CW :]

    pl.semaphore_wait(barrier, 15)

    red_copy = remote(red_out, red_in, red_s.at[0], red_r.at[0], {"row": mod(r - x + NROW, NROW)})

    @pl.when(x != 0)
    def _():
        red_copy.start()

    @pl.when(x == 0)
    def _():
        red_in[...] = red_out[...]

    redl_copies = [remote(redl.at[r], redl.at[r], redl_s, redl_r, row_id(k)) for k in (1, 2, 3)]
    for copy in redl_copies:
        copy.start()

    def band(columns, block):
        index = block * NROW + r
        near = jnp.concatenate(
            [
                ids_ref[pl.ds(jnp.maximum(index - 1, 0), 1), :],
                ids_ref[pl.ds(index, 1), :],
                ids_ref[pl.ds(jnp.minimum(index + 1, 63), 1), :],
            ],
            axis=1,
        )
        coef = jnp.zeros(near.shape, F32)
        for k in range(8):
            coef = jnp.where(near == k, kappa_ref[k], coef)
        coef = coef + 4.0
        here = coef[:, Q : 2 * Q]
        before = pltpu.roll(coef, 1, 1)[:, Q : 2 * Q]
        after = pltpu.roll(coef, 3 * Q - 1, 1)[:, Q : 2 * Q]
        row = index * Q + lanes((1, Q))
        ends = jnp.where((row == 0) | (row == 64 * Q - 1), 1.0, 2.0)
        off = row - columns
        return jnp.where(
            off == 0, here * here + ends,
            jnp.where(
                off == 1, -(here + before),
                jnp.where(off == -1, -(here + after), jnp.where(jnp.abs(off) == 2, 1.0, 0.0)),
            ),
        )

    load_dinv.wait()
    for k in range(2):
        d_hi, d_lo = split(dinv[k])
        gram = dg(d_hi, d_hi, 0, 0) + dg(d_hi, d_lo, 0, 0) + dg(d_lo, d_hi, 0, 0)
        g_hi, g_lo = split(gram)
        s_hi[k] = g_hi
        s_lo[k] = g_lo

    target = node_row // PW * Q + node_row % Q
    top_band = jnp.concatenate(
        [band(own_cols[:CW], 1), band(land_col, 0), band(land_col, 1)], axis=0
    )
    top_band = jnp.where(s == 0, top_band, 0.0)
    own_band = band(own_cols, s)

    @pl.when(x != 0)
    def _():
        red_copy.wait_recv()

    arrived(of_redl, redl_r)
    reduced_all = jnp.concatenate([red_in[...], redl[0] + redl[1] + redl[2] + redl[3]], axis=0)
    part = -mm(reduced_all, live_hi[...], live_lo[...], 0)
    part_hi, part_lo = split(part)
    pst[...] = jnp.concatenate([part_hi[: 2 * CW], part_lo[: 2 * CW]], axis=0)

    place_top = jnp.where(target == rows_of((2 * Q, 1)), 1.0, 0.0).astype(BF16)
    top = dg(jnp.concatenate([part_hi, part_lo], axis=0), place_top, 1, 1)
    top = top[: 2 * CW + NLAND] + top[2 * CW + NLAND :]
    top_out[...] = top_band + jnp.concatenate(
        [top[:CW, Q:], top[2 * CW :, :Q], top[2 * CW :, Q:]], axis=0
    )

    near_rows = 2 * CW // NEAR

    def quarter_rows(k):
        return pl.ds(pl.multiple_of(k * near_rows, near_rows), near_rows)

    near_copies = [
        remote(top_out.at[quarter_rows(mod(near + k, NEAR))], near_in.at[near], near_s, near_r, near_id(k))
        for k in (1, 2, 3)
    ]
    for copy in near_copies:
        copy.start()
    near_in[near] = top_out[quarter_rows(near), :]

    def contribution(block_a, block_b):
        place = rows_of((2 * Q, 1))
        place = jnp.where(place < Q, block_a * Q + place, block_b * Q + place - Q)
        place = jnp.where(target == place, 1.0, 0.0).astype(BF16)
        both = dg(pst[...], place, 1, 1)
        both = both[: 2 * CW] + both[2 * CW :]
        return both[:, :Q], both[:, Q:]

    def ring_copy(src, ring, send, recv, step, chunk, where):
        part_of = pl.ds(chunk * CROWS, CROWS)
        return pltpu.make_async_remote_copy(
            src_ref=src.at[part_of], dst_ref=ring.at[step, part_of],
            send_sem=send.at[step, chunk], recv_sem=recv.at[step, chunk],
            device_id=where, device_id_type=MESH,
        )

    def copy_p(src, step, chunk):
        return ring_copy(src, ring_p, rp_s, rp_r, step, chunk, right)

    def copy_m(src, step, chunk):
        return ring_copy(src, ring_m, rm_s, rm_r, step, chunk, left)

    to_right, to_left = contribution(mod(s + 8, NSUB), mod(s + 9, NSUB))
    first[0] = to_right
    first[1] = to_left
    for chunk in range(CHUNKS):
        copy_p(first.at[0], 0, chunk).start()
        copy_m(first.at[1], 0, chunk).start()

    def ring_step(t, carry):
        to_right, to_left = contribution(mod(s + 8 - t, NSUB), mod(s + 9 + t, NSUB))
        for chunk in range(CHUNKS):
            part_of = pl.ds(chunk * CROWS, CROWS)
            static = slice(chunk * CROWS, (chunk + 1) * CROWS)
            copy_p(ring_p.at[t - 1], t - 1, chunk).wait_recv()
            ring_p[t - 1, part_of, :] += to_right[static]
            copy_p(ring_p.at[t - 1], t, chunk).start()
            copy_m(ring_m.at[t - 1], t - 1, chunk).wait_recv()
            ring_m[t - 1, part_of, :] += to_left[static]
            copy_m(ring_m.at[t - 1], t, chunk).start()
        return carry

    lax.fori_loop(1, 2, ring_step, 0)
    arrived(of_near, near_r)
    near_sum[...] = near_in[0] + near_in[1] + near_in[2] + near_in[3]
    far_copies = [remote(near_sum, far_in.at[far], far_s, far_r, far_id(k)) for k in (1, 2, 3)]
    for copy in far_copies:
        copy.start()
    far_in[far] = near_sum[...]

    lax.fori_loop(2, 3, ring_step, 0)
    arrived(of_far, far_r)
    near_all[...] = far_in[0] + far_in[1] + far_in[2] + far_in[3]
    all_copies = [remote(near_all, top_all.at[quarter_rows(near)], all_s, all_r, near_id(k)) for k in (1, 2, 3)]
    for copy in all_copies:
        copy.start()
    top_all[quarter_rows(near), :] = near_all[...]

    lax.fori_loop(3, 4, ring_step, 0)
    arrived(of_all, all_r)

    row_copies = [remote(top_all.at[pl.ds(0, CW)], front_top.at[h, x, r], fy_s, fy_r, row_id(k)) for k in (1, 2, 3)]
    rland_copies = [
        remote(top_all.at[pl.ds(CW, 2 * NLAND)], rland.at[r], rl_s, rl_r, row_id(k)) for k in (1, 2, 3)
    ]
    for copy in row_copies + rland_copies:
        copy.start()
    front_top[h, x, r] = top_all[:CW]
    rland[r] = top_all[CW:]

    def x_copy(src_x, dst_x, where):
        return remote(front_top.at[h, src_x], front_top.at[h, src_x], fx_s.at[dst_x], fx_r.at[src_x], where)

    def fwd_copy(src_x, core):
        return remote(front_top.at[core, src_x], front_top.at[core, src_x], fwd_s.at[src_x], fwd_r.at[src_x], other)

    lax.fori_loop(4, 5, ring_step, 0)
    arrived(of_row, fy_r)
    x_copies = [x_copy(x, mod(x + k, 4), x_id(k)) for k in (1, 2, 3)]
    for copy in x_copies:
        copy.start()
    fwd_copy(x, h).start()

    lax.fori_loop(5, 7, ring_step, 0)
    for k in (1, 3, 2):
        from_x = mod(x + k, 4)
        x_copy(from_x, x, other).wait_recv()
        fwd_copy(from_x, h).start()

    to_right, own = contribution(mod(s + 1, NSUB), s)
    for chunk in range(CHUNKS):
        part_of = pl.ds(chunk * CROWS, CROWS)
        static = slice(chunk * CROWS, (chunk + 1) * CROWS)
        copy_p(ring_p.at[6], 6, chunk).wait_recv()
        ring_p[6, part_of, :] += to_right[static]
        copy_p(ring_p.at[6], 7, chunk).start()
    own = own + own_band
    for chunk in range(CHUNKS):
        part_of = pl.ds(chunk * CROWS, CROWS)
        static = slice(chunk * CROWS, (chunk + 1) * CROWS)
        copy_m(ring_m.at[6], 6, chunk).wait_recv()
        copy_p(ring_p.at[7], 7, chunk).wait_recv()
        fx[group, part_of, :] = own[static] + ring_m[6, part_of, :] + ring_p[7, part_of, :]

    def slot(px, ph):
        return 2 * mod(r + px, NROW) + ph

    def xag_copy(src_x, dst_x, where):
        return remote(fx.at[slot(src_x, h)], fx.at[slot(src_x, h)], xa_s.at[dst_x], xa_r.at[src_x], where)

    def xfwd_copy(px, ph):
        return remote(fx.at[slot(px, ph)], fx.at[slot(px, ph)], xf_s.at[px], xf_r.at[px], other)

    xag_copies = [xag_copy(x, mod(x + k, 4), x_id(k)) for k in (1, 2, 3)]
    for copy in xag_copies:
        copy.start()
    xfwd_copy(x, h).start()

    for k in range(4):
        fwd_copy(k, 1 - h).wait_recv()
    arrived(of_rland, rl_r)
    f_hi, f_lo = split(
        jnp.concatenate(
            [
                jnp.concatenate([front_top[g % 2, (g // 2 - k) % 4, k] for g in range(NCOL)], axis=0)
                for k in range(NROW)
            ],
            axis=1,
        )
    )
    r0 = jnp.concatenate([rland[k, :NLAND] for k in range(NROW)], axis=1)
    r1 = jnp.concatenate([rland[k, NLAND:] for k in range(NROW)], axis=1)
    own_rows = pl.ds(pl.multiple_of(c * CW, CW), CW)
    d0_own = dinv[0, own_rows, :]
    d1_own = dinv[1, own_rows, :]
    w0 = mm(r0, s_hi[0], s_lo[0], 0)
    t1 = r1 - mm(w0, f_hi, f_lo, 0)
    w1 = mm(t1, s_hi[1], s_lo[1], 0)
    back = mm(jnp.concatenate([d1_own, w1], axis=0), f_hi, f_lo, 1)
    back = mm(back, s_hi[0], s_lo[0], 0)
    column = lanes((NLAND, PW))
    e0 = jnp.where(column == land_col, 1.0, 0.0)
    e1 = jnp.where(column + PW == land_col, 1.0, 0.0)
    left0 = jnp.concatenate([d0_own, -back[:CW], e0 - w0 + back[CW:]], axis=0)
    left1 = jnp.concatenate([d1_own, e1 - w1], axis=0)

    for k in (1, 3, 2):
        from_x = mod(x + k, 4)
        xag_copy(from_x, x, other).wait_recv()
        xfwd_copy(from_x, h).start()
    for k in range(4):
        xfwd_copy(k, 1 - h).wait_recv()
    f0_hi, f0_lo = split(jnp.concatenate([fx[k, :CW] for k in range(NCOL)], axis=0))
    f1_hi, f1_lo = split(jnp.concatenate([fx[k, CW:] for k in range(NCOL)], axis=0))
    out0 = mm(left0, f0_hi, f0_lo, 0)
    out1 = mm(left1, f1_hi, f1_lo, 0)
    row_in = s * PW + r * Q + lanes((CW, Q))
    col_in = c * CW + rows_of((CW, Q))
    pf_ref[:CW] = jnp.where(row_in >= col_in, out0[:CW], 0.0)
    pf_ref[CW:] = jnp.where(row_in - PW >= col_in, out0[CW : 2 * CW] + out1[:CW], 0.0)
    ls_ref[...] = out0[2 * CW :] + out1[CW:]

    own_quarter = pl.ds(pl.multiple_of(r * Q, Q), Q)

    @pl.when(s == 0)
    def _():
        d_hi, d_lo = split(dinv[0, own_quarter, :])
        ls_ref[...] = mm(r0, d_hi, d_lo, 1)

    @pl.when(s == 1)
    def _():
        d_hi, d_lo = split(dinv[1, own_quarter, :])
        ls_ref[...] = mm(t1, d_hi, d_lo, 1)

    @pl.when(x != 0)
    def _():
        red_copy.wait_send()

    for bytes_of, sem in (
        (of_redl, redl_s), (of_near, near_s), (of_far, far_s), (of_all, all_s), (of_row, fy_s), (of_rland, rl_s)
    ):
        departed(bytes_of, sem)
    for copy in x_copies + xag_copies:
        copy.wait_send()
    for k in range(4):
        fwd_copy(k, h).wait_send()
    for k in range(4):
        xfwd_copy(k, h).wait_send()
    for chunk in range(CHUNKS):
        copy_p(first.at[0], 0, chunk).wait_send()
        copy_m(first.at[1], 0, chunk).wait_send()

        def sent_ring(t, carry):
            copy_p(ring_p.at[t - 1], t, chunk).wait_send()
            copy_m(ring_m.at[t - 1], t, chunk).wait_send()
            return carry

        lax.fori_loop(1, 7, sent_ring, 0)
        copy_p(ring_p.at[6], 7, chunk).wait_send()


def on_device(child_factor, child_map, child_len, class_ids, class_kappa, landmarks, diag_inverse):
    vmem = pl.BlockSpec(memory_space=pltpu.VMEM)
    hbm = pl.BlockSpec(memory_space=pltpu.HBM)
    dma = pltpu.SemaphoreType.DMA
    tile = (2 * CW, Q)
    panel_factor, landmark_solution = pl.pallas_call(
        kernel,
        out_shape=(
            jax.ShapeDtypeStruct((2 * CW, Q), F32),
            jax.ShapeDtypeStruct((NLAND, Q), F32),
        ),
        in_specs=[hbm] * 7,
        out_specs=(vmem, vmem),
        scratch_shapes=[
            pltpu.VMEM((1, NROW * NODEQ), jnp.int32),
            pltpu.SMEM((1,), jnp.int32),
            pltpu.VMEM((64, Q), jnp.int32),
            pltpu.SMEM((8,), F32),
            pltpu.VMEM((1, 256), jnp.int32),
            pltpu.VMEM((KCH, NODEQ), F32),
            pltpu.VMEM((2, PW, PW), F32),
            pltpu.VMEM((KCH, NODEQ), BF16),
            pltpu.VMEM((KCH, NODEQ), BF16),
            pltpu.VMEM((2 * CW, KCH), F32),
            pltpu.VMEM((2 * CW, KCH), F32),
            pltpu.VMEM((NROW, NLAND, KCH), F32),
            pltpu.VMEM((4 * CW, NODEQ), BF16),
            pltpu.VMEM(tile, F32),
            pltpu.VMEM((NEAR, 2 * CW // NEAR, Q), F32),
            pltpu.VMEM((2 * CW // NEAR, Q), F32),
            pltpu.VMEM((NEAR, 2 * CW // NEAR, Q), F32),
            pltpu.VMEM((2 * CW // NEAR, Q), F32),
            pltpu.VMEM(tile, F32),
            pltpu.VMEM((2, 4, NROW, CW, Q), F32),
            pltpu.VMEM((NROW, 2 * NLAND, Q), F32),
            pltpu.VMEM((2, PW, PW), BF16),
            pltpu.VMEM((2, PW, PW), BF16),
            pltpu.VMEM((2,) + tile, F32),
            pltpu.VMEM((8,) + tile, F32),
            pltpu.VMEM((7,) + tile, F32),
            pltpu.VMEM((NCOL,) + tile, F32),
            dma((7,)), dma((1,)), dma((1,)), dma, dma,
            dma, dma, dma, dma, dma, dma,
            dma, dma, dma((4,)), dma((4,)), dma((4,)), dma((4,)), dma, dma,
            dma((8, CHUNKS)), dma((8, CHUNKS)), dma((8, CHUNKS)), dma((8, CHUNKS)),
            dma((4,)), dma((4,)), dma((4,)), dma((4,)),
        ],
        compiler_params=pltpu.CompilerParams(
            collective_id=0, has_side_effects=True, vmem_limit_bytes=63 << 20
        ),
    )(
        child_factor, child_map, child_len, class_ids.reshape(64, Q), class_kappa,
        landmarks.reshape(1, 256), diag_inverse,
    )
    return panel_factor.reshape(2, CW, 1, Q), landmark_solution.reshape(NLAND, 1, Q)


def solution(mesh):
    return jax.shard_map(
        on_device,
        mesh=mesh,
        in_specs=(P("sub", None, "row"), P("sub", None), P("sub"), P(), P(), P(), P()),
        out_specs=(P(None, "col", "sub", "row"), P("col", "sub", "row")),
        check_vma=False,
    )
```

```python
import jax
import jax.numpy as jnp
from jax import lax
from jax.experimental import pallas as pl
from jax.experimental.pallas import tpu as pltpu
from jax.sharding import PartitionSpec as P

F32 = jnp.float32
BF16 = jnp.bfloat16
MESH = pl.DeviceIdType.MESH

NSUB, NROW, NCOL = 16, 4, 8
NEAR = 4
ORDER = (1, 4, 5, 6, 7)
PW, Q, CW, KCH, NODEQ, NLAND = 512, 128, 64, 256, 512, 32
CHUNKS = 2
CROWS = 2 * CW // CHUNKS


def dg(a, b, ca, cb):
    return lax.dot_general(a, b, (((ca,), (cb,)), ((), ())), preferred_element_type=F32)


def split(x):
    hi = x.astype(BF16)
    return hi, (x - hi.astype(F32)).astype(BF16)


def mm(a, b_hi, b_lo, cb):
    n = a.shape[0]
    a_hi, a_lo = split(a)
    both = dg(jnp.concatenate([a_hi, a_lo], axis=0), b_hi, 1, cb)
    return both[:n] + both[n:] + dg(a_hi, b_lo, 1, cb)


def mod(a, n):
    return lax.rem(a, jnp.int32(n))


def lanes(shape):
    return lax.broadcasted_iota(jnp.int32, shape, 1)


def rows_of(shape):
    return lax.broadcasted_iota(jnp.int32, shape, 0)


def kernel(
    factor_hbm, map_hbm, len_hbm, ids_hbm, kappa_hbm, land_hbm, dinv_hbm,
    out_ref,
    map_ref, len_ref, ids_ref, kappa_ref, land_ref, factor, dinv, live_hi, live_lo, red_out, red_in, redl, pst,
    top_out, near_in, near_sum, far_in, near_all, top_all, front_top, rland, s_hi, s_lo,
    first, ring_p, ring_m, fx,
    ld_sem, red_s, red_r, redl_s, redl_r, near_s, near_r, far_s, far_r, all_s, all_r,
    fy_s, fy_r, fx_s, fx_r, fwd_s, fwd_r, rl_s, rl_r,
    rp_s, rp_r, rm_s, rm_r, xa_s, xa_r, xf_s, xf_r,
):
    s = lax.axis_index("sub")
    r = lax.axis_index("row")
    c = lax.axis_index("col")
    x, h = lax.div(c, 2), mod(c, 2)
    far, near = lax.div(s, NEAR), mod(s, NEAR)
    other = {"col": 2 * x + 1 - h}
    group = 2 * mod(r + x, NROW) + h
    right = {"sub": mod(s + 1, NSUB)}
    left = {"sub": mod(s + NSUB - 1, NSUB)}

    def near_id(k):
        return {"sub": far * NEAR + mod(near + k, NEAR)}

    def far_id(k):
        return {"sub": mod(s + k * NEAR, NSUB)}

    def row_id(k):
        return {"row": mod(r + k, NROW)}

    def x_id(k):
        return {"col": 2 * mod(x + k, 4) + h}

    def remote(src, dst, send, recv, where):
        return pltpu.make_async_remote_copy(
            src_ref=src, dst_ref=dst, send_sem=send, recv_sem=recv, device_id=where, device_id_type=MESH
        )

    three = pl.ds(0, 3)
    of_redl, of_near, of_far = redl.at[three], near_in.at[three], far_in.at[three]
    of_all, of_row, of_rland = top_all.at[pl.ds(0, 3 * 2 * CW // NEAR)], front_top.at[0, 0, three], rland.at[three]

    def arrived(bytes_of, sem):
        remote(bytes_of, bytes_of, sem, sem, other).wait_recv()

    def departed(bytes_of, sem):
        remote(bytes_of, bytes_of, sem, sem, other).wait_send()

    load_factor = pltpu.make_async_copy(factor_hbm.at[0], factor, ld_sem.at[0])
    load_factor.start()
    small = [
        pltpu.make_async_copy(src, dst, ld_sem.at[2 + k])
        for k, (src, dst) in enumerate(
            [(map_hbm, map_ref), (land_hbm, land_ref), (len_hbm, len_ref), (ids_hbm, ids_ref), (kappa_hbm, kappa_ref)]
        )
    ]
    for copy in small:
        copy.start()
    load_dinv = pltpu.make_async_copy(dinv_hbm, dinv, ld_sem.at[1])
    load_dinv.start()
    barrier = pltpu.get_barrier_semaphore()

    for peer in [right, left, other] + [make(k) for make in (near_id, far_id, row_id, x_id) for k in (1, 2, 3)]:
        pl.semaphore_signal(barrier, inc=1, device_id=peer, device_id_type=MESH)

    for copy in small:
        copy.wait()
    node_row = map_ref[:, pl.ds(pl.multiple_of(r * NODEQ, NODEQ), NODEQ)]
    land_row = land_ref[...]
    land_col = jnp.sum(
        jnp.where(lanes((NLAND, 256)) == rows_of((NLAND, 256)) + c * NLAND, land_row.astype(F32), 0.0),
        axis=1, keepdims=True,
    ).astype(jnp.int32)
    iota_col = rows_of((2 * CW, 1))
    send_cols = iota_col // CW * PW + (2 * r + h) * CW + iota_col % CW
    own_cols = iota_col // CW * PW + group * CW + iota_col % CW
    select = jnp.concatenate([send_cols, land_col], axis=0) == node_row
    select = jnp.where(select, 1.0, 0.0).astype(BF16)
    load_factor.wait()
    live = jnp.where(lanes((KCH, NODEQ)) + r * NODEQ < len_ref[0], factor[...], 0.0)
    lh, ll = split(live)
    live_hi[...] = lh
    live_lo[...] = ll
    reduced = dg(select, lh, 1, 1) + dg(select, ll, 1, 1)
    red_out[...] = reduced[: 2 * CW]
    redl[r] = reduced[2 * CW :]

    pl.semaphore_wait(barrier, 15)

    red_copy = remote(red_out, red_in, red_s.at[0], red_r.at[0], {"row": mod(r - x + NROW, NROW)})

    @pl.when(x != 0)
    def _():
        red_copy.start()

    @pl.when(x == 0)
    def _():
        red_in[...] = red_out[...]

    redl_copies = [remote(redl.at[r], redl.at[r], redl_s, redl_r, row_id(k)) for k in (1, 2, 3)]
    for copy in redl_copies:
        copy.start()

    def band(columns, block):
        index = block * NROW + r
        near = jnp.concatenate(
            [
                ids_ref[pl.ds(jnp.maximum(index - 1, 0), 1), :],
                ids_ref[pl.ds(index, 1), :],
                ids_ref[pl.ds(jnp.minimum(index + 1, 63), 1), :],
            ],
            axis=1,
        )
        coef = jnp.zeros(near.shape, F32)
        for k in range(8):
            coef = jnp.where(near == k, kappa_ref[k], coef)
        coef = coef + 4.0
        here = coef[:, Q : 2 * Q]
        before = pltpu.roll(coef, 1, 1)[:, Q : 2 * Q]
        after = pltpu.roll(coef, 3 * Q - 1, 1)[:, Q : 2 * Q]
        row = index * Q + lanes((1, Q))
        ends = jnp.where((row == 0) | (row == 64 * Q - 1), 1.0, 2.0)
        off = row - columns
        return jnp.where(
            off == 0, here * here + ends,
            jnp.where(
                off == 1, -(here + before),
                jnp.where(off == -1, -(here + after), jnp.where(jnp.abs(off) == 2, 1.0, 0.0)),
            ),
        )

    load_dinv.wait()
    for k in range(2):
        d_hi, d_lo = split(dinv[k])
        gram = dg(d_hi, d_hi, 0, 0) + dg(d_hi, d_lo, 0, 0) + dg(d_lo, d_hi, 0, 0)
        g_hi, g_lo = split(gram)
        s_hi[k] = g_hi
        s_lo[k] = g_lo

    target = node_row // PW * Q + node_row % Q
    top_band = jnp.concatenate(
        [band(own_cols[:CW], 1), band(land_col, 0), band(land_col, 1)], axis=0
    )
    top_band = jnp.where(s == 0, top_band, 0.0)
    own_band = band(own_cols, s)

    @pl.when(x != 0)
    def _():
        red_copy.wait_recv()

    arrived(of_redl, redl_r)
    reduced_all = jnp.concatenate([red_in[...], redl[0] + redl[1] + redl[2] + redl[3]], axis=0)
    part = -mm(reduced_all, live_hi[...], live_lo[...], 0)
    part_hi, part_lo = split(part)
    pst[...] = jnp.concatenate([part_hi[: 2 * CW], part_lo[: 2 * CW]], axis=0)

    place_top = jnp.where(target == rows_of((2 * Q, 1)), 1.0, 0.0).astype(BF16)
    top = dg(jnp.concatenate([part_hi, part_lo], axis=0), place_top, 1, 1)
    top = top[: 2 * CW + NLAND] + top[2 * CW + NLAND :]
    top_out[...] = top_band + jnp.concatenate(
        [top[:CW, Q:], top[2 * CW :, :Q], top[2 * CW :, Q:]], axis=0
    )

    near_rows = 2 * CW // NEAR

    def quarter_rows(k):
        return pl.ds(pl.multiple_of(k * near_rows, near_rows), near_rows)

    near_copies = [
        remote(top_out.at[quarter_rows(mod(near + k, NEAR))], near_in.at[near], near_s, near_r, near_id(k))
        for k in (1, 2, 3)
    ]
    for copy in near_copies:
        copy.start()
    near_in[near] = top_out[quarter_rows(near), :]

    def contribution(block_a, block_b):
        place = rows_of((2 * Q, 1))
        place = jnp.where(place < Q, block_a * Q + place, block_b * Q + place - Q)
        place = jnp.where(target == place, 1.0, 0.0).astype(BF16)
        both = dg(pst[...], place, 1, 1)
        both = both[: 2 * CW] + both[2 * CW :]
        return both[:, :Q], both[:, Q:]

    def ring_copy(src, ring, send, recv, step, chunk, where):
        part_of = pl.ds(chunk * CROWS, CROWS)
        return pltpu.make_async_remote_copy(
            src_ref=src.at[part_of], dst_ref=ring.at[step, part_of],
            send_sem=send.at[step, chunk], recv_sem=recv.at[step, chunk],
            device_id=where, device_id_type=MESH,
        )

    def copy_p(src, step, chunk):
        return ring_copy(src, ring_p, rp_s, rp_r, step, chunk, right)

    def copy_m(src, step, chunk):
        return ring_copy(src, ring_m, rm_s, rm_r, step, chunk, left)

    to_right, to_left = contribution(mod(s + 8, NSUB), mod(s + 9, NSUB))
    first[0] = to_right
    first[1] = to_left
    for chunk in range(CHUNKS):
        copy_p(first.at[0], 0, chunk).start()
        copy_m(first.at[1], 0, chunk).start()

    def ring_step(t, carry):
        to_right, to_left = contribution(mod(s + 8 - t, NSUB), mod(s + 9 + t, NSUB))
        for chunk in range(CHUNKS):
            part_of = pl.ds(chunk * CROWS, CROWS)
            static = slice(chunk * CROWS, (chunk + 1) * CROWS)
            copy_p(ring_p.at[t - 1], t - 1, chunk).wait_recv()
            ring_p[t - 1, part_of, :] += to_right[static]
            copy_p(ring_p.at[t - 1], t, chunk).start()
            copy_m(ring_m.at[t - 1], t - 1, chunk).wait_recv()
            ring_m[t - 1, part_of, :] += to_left[static]
            copy_m(ring_m.at[t - 1], t, chunk).start()
        return carry

    far_copies = [remote(near_sum, far_in.at[far], far_s, far_r, far_id(k)) for k in (1, 2, 3)]
    all_copies = [remote(near_all, top_all.at[quarter_rows(near)], all_s, all_r, near_id(k)) for k in (1, 2, 3)]
    row_copies = [remote(top_all.at[pl.ds(0, CW)], front_top.at[h, x, r], fy_s, fy_r, row_id(k)) for k in (1, 2, 3)]
    rland_copies = [
        remote(top_all.at[pl.ds(CW, 2 * NLAND)], rland.at[r], rl_s, rl_r, row_id(k)) for k in (1, 2, 3)
    ]

    def x_copy(src_x, dst_x, where):
        return remote(front_top.at[h, src_x], front_top.at[h, src_x], fx_s.at[dst_x], fx_r.at[src_x], where)

    def fwd_copy(src_x, core):
        return remote(front_top.at[core, src_x], front_top.at[core, src_x], fwd_s.at[src_x], fwd_r.at[src_x], other)

    x_copies = [x_copy(x, mod(x + k, 4), x_id(k)) for k in (1, 2, 3)]

    def near_step():
        arrived(of_near, near_r)
        near_sum[...] = near_in[0] + near_in[1] + near_in[2] + near_in[3]
        for copy in far_copies:
            copy.start()
        far_in[far] = near_sum[...]

    def far_step():
        arrived(of_far, far_r)
        near_all[...] = far_in[0] + far_in[1] + far_in[2] + far_in[3]
        for copy in all_copies:
            copy.start()
        top_all[quarter_rows(near), :] = near_all[...]

    def all_step():
        arrived(of_all, all_r)
        for copy in row_copies + rland_copies:
            copy.start()
        front_top[h, x, r] = top_all[:CW]
        rland[r] = top_all[CW:]

    def row_step():
        arrived(of_row, fy_r)
        for copy in x_copies:
            copy.start()
        fwd_copy(x, h).start()

    def x_step():
        for k in (1, 3, 2):
            from_x = mod(x + k, 4)
            x_copy(from_x, x, other).wait_recv()
            fwd_copy(from_x, h).start()

    done = 1
    for top_step, ring_done in zip((near_step, far_step, all_step, row_step, x_step), ORDER):
        if min(ring_done, 6) >= done:
            lax.fori_loop(done, min(ring_done, 6) + 1, ring_step, 0)
            done = min(ring_done, 6) + 1
        if ring_done < 7:
            top_step()
    if done < 7:
        lax.fori_loop(done, 7, ring_step, 0)

    to_right, own = contribution(mod(s + 1, NSUB), s)
    for chunk in range(CHUNKS):
        part_of = pl.ds(chunk * CROWS, CROWS)
        static = slice(chunk * CROWS, (chunk + 1) * CROWS)
        copy_p(ring_p.at[6], 6, chunk).wait_recv()
        ring_p[6, part_of, :] += to_right[static]
        copy_p(ring_p.at[6], 7, chunk).start()
    own = own + own_band
    for chunk in range(CHUNKS):
        part_of = pl.ds(chunk * CROWS, CROWS)
        static = slice(chunk * CROWS, (chunk + 1) * CROWS)
        copy_m(ring_m.at[6], 6, chunk).wait_recv()
        copy_p(ring_p.at[7], 7, chunk).wait_recv()
        fx[group, part_of, :] = own[static] + ring_m[6, part_of, :] + ring_p[7, part_of, :]

    def slot(px, ph):
        return 2 * mod(r + px, NROW) + ph

    def xag_copy(src_x, dst_x, where):
        return remote(fx.at[slot(src_x, h)], fx.at[slot(src_x, h)], xa_s.at[dst_x], xa_r.at[src_x], where)

    def xfwd_copy(px, ph):
        return remote(fx.at[slot(px, ph)], fx.at[slot(px, ph)], xf_s.at[px], xf_r.at[px], other)

    xag_copies = [xag_copy(x, mod(x + k, 4), x_id(k)) for k in (1, 2, 3)]
    for copy in xag_copies:
        copy.start()
    xfwd_copy(x, h).start()

    for top_step, ring_done in zip((near_step, far_step, all_step, row_step, x_step), ORDER):
        if ring_done == 7:
            top_step()

    for k in range(4):
        fwd_copy(k, 1 - h).wait_recv()
    arrived(of_rland, rl_r)
    f_hi, f_lo = split(
        jnp.concatenate(
            [
                jnp.concatenate([front_top[g % 2, (g // 2 - k) % 4, k] for g in range(NCOL)], axis=0)
                for k in range(NROW)
            ],
            axis=1,
        )
    )
    r0 = jnp.concatenate([rland[k, :NLAND] for k in range(NROW)], axis=1)
    r1 = jnp.concatenate([rland[k, NLAND:] for k in range(NROW)], axis=1)
    own_rows = pl.ds(pl.multiple_of(c * CW, CW), CW)
    d0_own = dinv[0, own_rows, :]
    d1_own = dinv[1, own_rows, :]
    w0 = mm(r0, s_hi[0], s_lo[0], 0)
    t1 = r1 - mm(w0, f_hi, f_lo, 0)
    w1 = mm(t1, s_hi[1], s_lo[1], 0)
    back = mm(jnp.concatenate([d1_own, w1], axis=0), f_hi, f_lo, 1)
    back = mm(back, s_hi[0], s_lo[0], 0)
    column = lanes((NLAND, PW))
    e0 = jnp.where(column == land_col, 1.0, 0.0)
    e1 = jnp.where(column + PW == land_col, 1.0, 0.0)
    left0 = jnp.concatenate([d0_own, -back[:CW], e0 - w0 + back[CW:]], axis=0)
    left1 = jnp.concatenate([d1_own, e1 - w1], axis=0)

    for k in (1, 3, 2):
        from_x = mod(x + k, 4)
        xag_copy(from_x, x, other).wait_recv()
        xfwd_copy(from_x, h).start()
    for k in range(4):
        xfwd_copy(k, 1 - h).wait_recv()
    f0_hi, f0_lo = split(jnp.concatenate([fx[k, :CW] for k in range(NCOL)], axis=0))
    f1_hi, f1_lo = split(jnp.concatenate([fx[k, CW:] for k in range(NCOL)], axis=0))
    out0 = mm(left0, f0_hi, f0_lo, 0)
    out1 = mm(left1, f1_hi, f1_lo, 0)
    row_in = s * PW + r * Q + lanes((CW, Q))
    col_in = c * CW + rows_of((CW, Q))
    out_ref[:CW] = jnp.where(row_in >= col_in, out0[:CW], 0.0)
    out_ref[CW : 2 * CW] = jnp.where(row_in - PW >= col_in, out0[CW : 2 * CW] + out1[:CW], 0.0)
    out_ref[2 * CW :] = out0[2 * CW :] + out1[CW:]

    own_quarter = pl.ds(pl.multiple_of(r * Q, Q), Q)

    @pl.when(s == 0)
    def _():
        d_hi, d_lo = split(dinv[0, own_quarter, :])
        out_ref[2 * CW :] = mm(r0, d_hi, d_lo, 1)

    @pl.when(s == 1)
    def _():
        d_hi, d_lo = split(dinv[1, own_quarter, :])
        out_ref[2 * CW :] = mm(t1, d_hi, d_lo, 1)

    @pl.when(x != 0)
    def _():
        red_copy.wait_send()

    for bytes_of, sem in (
        (of_redl, redl_s), (of_near, near_s), (of_far, far_s), (of_all, all_s), (of_row, fy_s), (of_rland, rl_s)
    ):
        departed(bytes_of, sem)
    for copy in x_copies + xag_copies:
        copy.wait_send()
    for k in range(4):
        fwd_copy(k, h).wait_send()
    for k in range(4):
        xfwd_copy(k, h).wait_send()
    for chunk in range(CHUNKS):
        copy_p(first.at[0], 0, chunk).wait_send()
        copy_m(first.at[1], 0, chunk).wait_send()

        def sent_ring(t, carry):
            copy_p(ring_p.at[t - 1], t, chunk).wait_send()
            copy_m(ring_m.at[t - 1], t, chunk).wait_send()
            return carry

        lax.fori_loop(1, 7, sent_ring, 0)
        copy_p(ring_p.at[6], 7, chunk).wait_send()


def on_device(child_factor, child_map, child_len, class_ids, class_kappa, landmarks, diag_inverse):
    vmem = pl.BlockSpec(memory_space=pltpu.VMEM)
    hbm = pl.BlockSpec(memory_space=pltpu.HBM)
    dma = pltpu.SemaphoreType.DMA
    tile = (2 * CW, Q)
    out = pl.pallas_call(
        kernel,
        out_shape=pltpu.VMEM((2 * CW + NLAND, Q), F32),
        in_specs=[hbm] * 7,
        out_specs=vmem,
        scratch_shapes=[
            pltpu.VMEM((1, NROW * NODEQ), jnp.int32),
            pltpu.SMEM((1,), jnp.int32),
            pltpu.VMEM((64, Q), jnp.int32),
            pltpu.SMEM((8,), F32),
            pltpu.VMEM((1, 256), jnp.int32),
            pltpu.VMEM((KCH, NODEQ), F32),
            pltpu.VMEM((2, PW, PW), F32),
            pltpu.VMEM((KCH, NODEQ), BF16),
            pltpu.VMEM((KCH, NODEQ), BF16),
            pltpu.VMEM((2 * CW, KCH), F32),
            pltpu.VMEM((2 * CW, KCH), F32),
            pltpu.VMEM((NROW, NLAND, KCH), F32),
            pltpu.VMEM((4 * CW, NODEQ), BF16),
            pltpu.VMEM(tile, F32),
            pltpu.VMEM((NEAR, 2 * CW // NEAR, Q), F32),
            pltpu.VMEM((2 * CW // NEAR, Q), F32),
            pltpu.VMEM((NEAR, 2 * CW // NEAR, Q), F32),
            pltpu.VMEM((2 * CW // NEAR, Q), F32),
            pltpu.VMEM(tile, F32),
            pltpu.VMEM((2, 4, NROW, CW, Q), F32),
            pltpu.VMEM((NROW, 2 * NLAND, Q), F32),
            pltpu.VMEM((2, PW, PW), BF16),
            pltpu.VMEM((2, PW, PW), BF16),
            pltpu.VMEM((2,) + tile, F32),
            pltpu.VMEM((8,) + tile, F32),
            pltpu.VMEM((7,) + tile, F32),
            pltpu.VMEM((NCOL,) + tile, F32),
            dma((7,)), dma((1,)), dma((1,)), dma, dma,
            dma, dma, dma, dma, dma, dma,
            dma, dma, dma((4,)), dma((4,)), dma((4,)), dma((4,)), dma, dma,
            dma((8, CHUNKS)), dma((8, CHUNKS)), dma((8, CHUNKS)), dma((8, CHUNKS)),
            dma((4,)), dma((4,)), dma((4,)), dma((4,)),
        ],
        compiler_params=pltpu.CompilerParams(
            collective_id=0, has_side_effects=True, vmem_limit_bytes=63 << 20
        ),
    )(
        child_factor, child_map, child_len, class_ids.reshape(64, Q), class_kappa,
        landmarks.reshape(1, 256), diag_inverse,
    )
    return out[: 2 * CW].reshape(2, CW, 1, Q), out[2 * CW :].reshape(NLAND, 1, Q)


def solution(mesh):
    return jax.shard_map(
        on_device,
        mesh=mesh,
        in_specs=(P("sub", None, "row"), P("sub", None), P("sub"), P(), P(), P(), P()),
        out_specs=(P(None, "col", "sub", "row"), P("col", "sub", "row")),
        check_vma=False,
    )
```

```python
import jax
import jax.numpy as jnp
from jax import lax
from jax.experimental import pallas as pl
from jax.experimental.pallas import tpu as pltpu
from jax.sharding import PartitionSpec as P

F32 = jnp.float32
BF16 = jnp.bfloat16
MESH = pl.DeviceIdType.MESH

NSUB, NROW, NCOL = 16, 4, 8
NEAR = 4
ORDER = (1, 2, 3, 4, 5)
PW, Q, CW, KCH, NODEQ, NLAND = 512, 128, 64, 256, 512, 32


def dg(a, b, ca, cb):
    return lax.dot_general(a, b, (((ca,), (cb,)), ((), ())), preferred_element_type=F32)


def split(x):
    hi = x.astype(BF16)
    return hi, (x - hi.astype(F32)).astype(BF16)


def mm(a, b_hi, b_lo, cb):
    n = a.shape[0]
    a_hi, a_lo = split(a)
    both = dg(jnp.concatenate([a_hi, a_lo], axis=0), b_hi, 1, cb)
    return both[:n] + both[n:] + dg(a_hi, b_lo, 1, cb)


def mod(a, n):
    return lax.rem(a, jnp.int32(n))


def lanes(shape):
    return lax.broadcasted_iota(jnp.int32, shape, 1)


def rows_of(shape):
    return lax.broadcasted_iota(jnp.int32, shape, 0)


def kernel(
    factor_hbm, map_hbm, len_hbm, ids_hbm, kappa_hbm, land_hbm, dinv_hbm,
    out_ref,
    map_ref, len_ref, ids_ref, kappa_ref, land_ref, factor, dinv, live_hi, live_lo, red_out, red_in, redl, pst,
    top_out, near_in, near_sum, far_in, near_all, top_all, front_top, rland, s_hi, s_lo,
    terms, pre_p, pre_m, go_p, go_m, fx,
    ld_sem, red_s, red_r, redl_s, redl_r, near_s, near_r, far_s, far_r, all_s, all_r,
    fy_s, fy_r, fc_s, fc_r, fx_s, fx_r, fwd_s, fwd_r, rl_s, rl_r,
    pp_s, pp_r, pm_s, pm_r, gp_s, gp_r, gm_s, gm_r, xa_s, xa_r, xf_s, xf_r,
):
    s = lax.axis_index("sub")
    r = lax.axis_index("row")
    c = lax.axis_index("col")
    x, h = lax.div(c, 2), mod(c, 2)
    far, near = lax.div(s, NEAR), mod(s, NEAR)
    other = {"col": 2 * x + 1 - h}
    group = 2 * mod(r + x, NROW) + h
    right = {"sub": mod(s + 1, NSUB)}
    left = {"sub": mod(s + NSUB - 1, NSUB)}
    right2 = {"sub": mod(s + 2, NSUB)}
    left2 = {"sub": mod(s + NSUB - 2, NSUB)}

    def near_id(k):
        return {"sub": far * NEAR + mod(near + k, NEAR)}

    def far_id(k):
        return {"sub": mod(s + k * NEAR, NSUB)}

    def row_id(k):
        return {"row": mod(r + k, NROW)}

    def x_id(k):
        return {"col": 2 * mod(x + k, 4) + h}

    def remote(src, dst, send, recv, where):
        return pltpu.make_async_remote_copy(
            src_ref=src, dst_ref=dst, send_sem=send, recv_sem=recv, device_id=where, device_id_type=MESH
        )

    three = pl.ds(0, 3)
    of_redl, of_near, of_far = redl.at[three], near_in.at[three], far_in.at[three]
    of_all, of_row, of_rland = top_all.at[pl.ds(0, 3 * 2 * CW // NEAR)], front_top.at[0, 0, 0, three], rland.at[three]

    def arrived(bytes_of, sem):
        remote(bytes_of, bytes_of, sem, sem, other).wait_recv()

    def departed(bytes_of, sem):
        remote(bytes_of, bytes_of, sem, sem, other).wait_send()

    load_factor = pltpu.make_async_copy(factor_hbm.at[0], factor, ld_sem.at[0])
    load_factor.start()
    small = [
        pltpu.make_async_copy(src, dst, ld_sem.at[2 + k])
        for k, (src, dst) in enumerate(
            [(map_hbm, map_ref), (land_hbm, land_ref), (len_hbm, len_ref), (ids_hbm, ids_ref), (kappa_hbm, kappa_ref)]
        )
    ]
    for copy in small:
        copy.start()
    load_dinv = pltpu.make_async_copy(dinv_hbm, dinv, ld_sem.at[1])
    load_dinv.start()
    barrier = pltpu.get_barrier_semaphore()

    for peer in [right, left, right2, left2, other] + [make(k) for make in (near_id, far_id, row_id, x_id) for k in (1, 2, 3)]:
        pl.semaphore_signal(barrier, inc=1, device_id=peer, device_id_type=MESH)

    for copy in small:
        copy.wait()
    node_row = map_ref[:, pl.ds(pl.multiple_of(r * NODEQ, NODEQ), NODEQ)]
    land_row = land_ref[...]
    land_col = jnp.sum(
        jnp.where(lanes((NLAND, 256)) == rows_of((NLAND, 256)) + c * NLAND, land_row.astype(F32), 0.0),
        axis=1, keepdims=True,
    ).astype(jnp.int32)
    iota_col = rows_of((2 * CW, 1))
    send_cols = iota_col // CW * PW + (2 * r + h) * CW + iota_col % CW
    own_cols = iota_col // CW * PW + group * CW + iota_col % CW
    select = jnp.concatenate([send_cols, land_col], axis=0) == node_row
    select = jnp.where(select, 1.0, 0.0).astype(BF16)
    load_factor.wait()
    live = jnp.where(lanes((KCH, NODEQ)) + r * NODEQ < len_ref[0], factor[...], 0.0)
    lh, ll = split(live)
    live_hi[...] = lh
    live_lo[...] = ll
    reduced = dg(select, lh, 1, 1) + dg(select, ll, 1, 1)
    red_out[...] = reduced[: 2 * CW]
    redl[r] = reduced[2 * CW :]

    pl.semaphore_wait(barrier, 17)

    red_copy = remote(red_out, red_in, red_s.at[0], red_r.at[0], {"row": mod(r - x + NROW, NROW)})

    @pl.when(x != 0)
    def _():
        red_copy.start()

    @pl.when(x == 0)
    def _():
        red_in[...] = red_out[...]

    redl_copies = [remote(redl.at[r], redl.at[r], redl_s, redl_r, row_id(k)) for k in (1, 2, 3)]
    for copy in redl_copies:
        copy.start()

    def band(columns, block):
        index = block * NROW + r
        near = jnp.concatenate(
            [
                ids_ref[pl.ds(jnp.maximum(index - 1, 0), 1), :],
                ids_ref[pl.ds(index, 1), :],
                ids_ref[pl.ds(jnp.minimum(index + 1, 63), 1), :],
            ],
            axis=1,
        )
        coef = jnp.zeros(near.shape, F32)
        for k in range(8):
            coef = jnp.where(near == k, kappa_ref[k], coef)
        coef = coef + 4.0
        here = coef[:, Q : 2 * Q]
        before = pltpu.roll(coef, 1, 1)[:, Q : 2 * Q]
        after = pltpu.roll(coef, 3 * Q - 1, 1)[:, Q : 2 * Q]
        row = index * Q + lanes((1, Q))
        ends = jnp.where((row == 0) | (row == 64 * Q - 1), 1.0, 2.0)
        off = row - columns
        return jnp.where(
            off == 0, here * here + ends,
            jnp.where(
                off == 1, -(here + before),
                jnp.where(off == -1, -(here + after), jnp.where(jnp.abs(off) == 2, 1.0, 0.0)),
            ),
        )

    load_dinv.wait()
    for k in range(2):
        d_hi, d_lo = split(dinv[k])
        gram = dg(d_hi, d_hi, 0, 0) + dg(d_hi, d_lo, 0, 0) + dg(d_lo, d_hi, 0, 0)
        g_hi, g_lo = split(gram)
        s_hi[k] = g_hi
        s_lo[k] = g_lo

    target = node_row // PW * Q + node_row % Q
    top_band = jnp.concatenate(
        [band(own_cols[:CW], 1), band(land_col, 0), band(land_col, 1)], axis=0
    )
    top_band = jnp.where(s == 0, top_band, 0.0)
    own_band = band(own_cols, s)

    @pl.when(x != 0)
    def _():
        red_copy.wait_recv()

    arrived(of_redl, redl_r)
    reduced_all = jnp.concatenate([red_in[...], redl[0] + redl[1] + redl[2] + redl[3]], axis=0)
    part = -mm(reduced_all, live_hi[...], live_lo[...], 0)
    part_hi, part_lo = split(part)
    pst[...] = jnp.concatenate([part_hi[: 2 * CW], part_lo[: 2 * CW]], axis=0)

    def term(k):
        block_a, block_b = mod(s + 8 - k, NSUB), mod(s + 9 + k, NSUB)
        place = rows_of((2 * Q, 1))
        place = jnp.where(place < Q, block_a * Q + place, block_b * Q + place - Q)
        place = jnp.where(target == place, 1.0, 0.0).astype(BF16)
        both = dg(pst[...], place, 1, 1)
        both = both[: 2 * CW] + both[2 * CW :]
        terms[k, 0] = both[:, :Q]
        terms[k, 1] = both[:, Q:]

    pair_p = [remote(terms.at[2 * k, 0], pre_p.at[k], pp_s.at[k], pp_r.at[k], right) for k in range(4)]
    pair_m = [remote(terms.at[2 * k + 1, 1], pre_m.at[k], pm_s.at[k], pm_r.at[k], left) for k in range(3)]
    sum_p = [remote(pre_p.at[k], go_p.at[k], gp_s.at[k], gp_r.at[k], right2 if k < 3 else right) for k in range(4)]
    sum_m = [remote(terms.at[0, 1], go_m.at[0], gm_s.at[0], gm_r.at[0], left2)] + [
        remote(pre_m.at[k - 1], go_m.at[k], gm_s.at[k], gm_r.at[k], left2 if k < 3 else left) for k in (1, 2, 3)
    ]

    def pass_p(k):
        pair_p[k].wait_recv()
        if k == 0:
            pre_p[k] += terms[1, 0]
        else:
            sum_p[k - 1].wait_recv()
            pre_p[k] += go_p[k - 1] + terms[2 * k + 1, 0]
        sum_p[k].start()

    def pass_m(k):
        pair_m[k - 1].wait_recv()
        sum_m[k - 1].wait_recv()
        pre_m[k - 1] += go_m[k - 1] + terms[2 * k, 1]
        sum_m[k].start()

    place_top = jnp.where(target == rows_of((2 * Q, 1)), 1.0, 0.0).astype(BF16)
    top = dg(jnp.concatenate([part_hi, part_lo], axis=0), place_top, 1, 1)
    top = top[: 2 * CW + NLAND] + top[2 * CW + NLAND :]
    top_out[...] = top_band + jnp.concatenate(
        [top[:CW, Q:], top[2 * CW :, :Q], top[2 * CW :, Q:]], axis=0
    )

    near_rows = 2 * CW // NEAR

    def quarter_rows(k):
        return pl.ds(pl.multiple_of(k * near_rows, near_rows), near_rows)

    near_copies = [
        remote(top_out.at[quarter_rows(mod(near + k, NEAR))], near_in.at[near], near_s, near_r, near_id(k))
        for k in (1, 2, 3)
    ]
    for copy in near_copies:
        copy.start()
    near_in[near] = top_out[quarter_rows(near), :]

    term(0)
    pair_p[0].start()
    sum_m[0].start()
    term(1)
    pair_m[0].start()
    term(2)
    pair_p[1].start()

    far_copies = [remote(near_sum, far_in.at[far], far_s, far_r, far_id(k)) for k in (1, 2, 3)]
    all_copies = [remote(near_all, top_all.at[quarter_rows(near)], all_s, all_r, near_id(k)) for k in (1, 2, 3)]
    half = CW // 2
    row_copies = [
        remote(top_all.at[pl.ds(0, half)], front_top.at[h, 0, x, r], fy_s, fy_r, row_id(k)) for k in (1, 2, 3)
    ]
    col_copies = [
        remote(top_all.at[pl.ds(half, half)], front_top.at[h, 1, r, x], fc_s, fc_r, x_id(k)) for k in (1, 2, 3)
    ]
    rland_copies = [
        remote(top_all.at[pl.ds(CW, 2 * NLAND)], rland.at[r], rl_s, rl_r, row_id(k)) for k in (1, 2, 3)
    ]

    def wide_copy(part, src, dst, where):
        piece = front_top.at[h, part, src]
        return remote(piece, piece, fx_s.at[part, dst], fx_r.at[part, src], where)

    def fwd_copy(part, src, core):
        piece = front_top.at[core, part, src]
        return remote(piece, piece, fwd_s.at[part, src], fwd_r.at[part, src], other)

    x_copies = [wide_copy(0, x, mod(x + k, 4), x_id(k)) for k in (1, 2, 3)]
    y_copies = [wide_copy(1, r, mod(r + k, 4), row_id(k)) for k in (1, 2, 3)]

    def near_step():
        arrived(of_near, near_r)
        near_sum[...] = near_in[0] + near_in[1] + near_in[2] + near_in[3]
        for copy in far_copies:
            copy.start()
        far_in[far] = near_sum[...]

    def far_step():
        arrived(of_far, far_r)
        near_all[...] = far_in[0] + far_in[1] + far_in[2] + far_in[3]
        for copy in all_copies:
            copy.start()
        top_all[quarter_rows(near), :] = near_all[...]

    def all_step():
        arrived(of_all, all_r)
        for copy in row_copies + col_copies + rland_copies:
            copy.start()
        front_top[h, 0, x, r] = top_all[:half]
        front_top[h, 1, r, x] = top_all[half:CW]
        rland[r] = top_all[CW:]

    def row_step():
        arrived(of_row, fy_r)
        for copy in x_copies:
            copy.start()
        arrived(of_row, fc_r)
        for copy in y_copies:
            copy.start()
        fwd_copy(0, x, h).start()
        fwd_copy(1, r, h).start()

    def x_step():
        for k in (1, 3, 2):
            from_x, from_row = mod(x + k, 4), mod(r + k, 4)
            wide_copy(0, from_x, x, other).wait_recv()
            fwd_copy(0, from_x, h).start()
            wide_copy(1, from_row, r, other).wait_recv()
            fwd_copy(1, from_row, h).start()

    top_steps = (near_step, far_step, all_step, row_step, x_step)

    def tops(step):
        for top_step, place in zip(top_steps, ORDER):
            if place == step:
                top_step()

    for step in range(4):
        pass_p(step)
        if step:
            pass_m(step)
        tops(step + 1)
        if step < 2:
            term(2 * step + 3)
            pair_m[step + 1].start()
            term(2 * step + 4)
            pair_p[step + 2].start()
        if step == 2:
            term(7)

    own = terms[7, 1] + own_band
    sum_m[3].wait_recv()
    sum_p[3].wait_recv()
    fx[group] = own + go_m[3] + go_p[3]

    def slot(px, ph):
        return 2 * mod(r + px, NROW) + ph

    def xag_copy(src_x, dst_x, where):
        return remote(fx.at[slot(src_x, h)], fx.at[slot(src_x, h)], xa_s.at[dst_x], xa_r.at[src_x], where)

    def xfwd_copy(px, ph):
        return remote(fx.at[slot(px, ph)], fx.at[slot(px, ph)], xf_s.at[px], xf_r.at[px], other)

    xag_copies = [xag_copy(x, mod(x + k, 4), x_id(k)) for k in (1, 2, 3)]
    for copy in xag_copies:
        copy.start()
    xfwd_copy(x, h).start()

    tops(5)

    for k in range(4):
        fwd_copy(0, k, 1 - h).wait_recv()
        fwd_copy(1, k, 1 - h).wait_recv()
    arrived(of_rland, rl_r)
    f_hi, f_lo = split(
        jnp.concatenate(
            [
                jnp.concatenate(
                    [
                        piece
                        for g in range(NCOL)
                        for piece in (
                            front_top[g % 2, 0, (g // 2 - k) % 4, k], front_top[g % 2, 1, k, (g // 2 - k) % 4]
                        )
                    ],
                    axis=0,
                )
                for k in range(NROW)
            ],
            axis=1,
        )
    )
    r0 = jnp.concatenate([rland[k, :NLAND] for k in range(NROW)], axis=1)
    r1 = jnp.concatenate([rland[k, NLAND:] for k in range(NROW)], axis=1)
    own_rows = pl.ds(pl.multiple_of(c * CW, CW), CW)
    d0_own = dinv[0, own_rows, :]
    d1_own = dinv[1, own_rows, :]
    w0 = mm(r0, s_hi[0], s_lo[0], 0)
    t1 = r1 - mm(w0, f_hi, f_lo, 0)
    w1 = mm(t1, s_hi[1], s_lo[1], 0)
    back = mm(jnp.concatenate([d1_own, w1], axis=0), f_hi, f_lo, 1)
    back = mm(back, s_hi[0], s_lo[0], 0)
    column = lanes((NLAND, PW))
    e0 = jnp.where(column == land_col, 1.0, 0.0)
    e1 = jnp.where(column + PW == land_col, 1.0, 0.0)
    left0 = jnp.concatenate([d0_own, -back[:CW], e0 - w0 + back[CW:]], axis=0)
    left1 = jnp.concatenate([d1_own, e1 - w1], axis=0)

    for k in (1, 3, 2):
        from_x = mod(x + k, 4)
        xag_copy(from_x, x, other).wait_recv()
        xfwd_copy(from_x, h).start()
    for k in range(4):
        xfwd_copy(k, 1 - h).wait_recv()
    f0_hi, f0_lo = split(jnp.concatenate([fx[k, :CW] for k in range(NCOL)], axis=0))
    f1_hi, f1_lo = split(jnp.concatenate([fx[k, CW:] for k in range(NCOL)], axis=0))
    out0 = mm(left0, f0_hi, f0_lo, 0)
    out1 = mm(left1, f1_hi, f1_lo, 0)
    row_in = s * PW + r * Q + lanes((CW, Q))
    col_in = c * CW + rows_of((CW, Q))
    out_ref[:CW] = jnp.where(row_in >= col_in, out0[:CW], 0.0)
    out_ref[CW : 2 * CW] = jnp.where(row_in - PW >= col_in, out0[CW : 2 * CW] + out1[:CW], 0.0)
    out_ref[2 * CW :] = out0[2 * CW :] + out1[CW:]

    own_quarter = pl.ds(pl.multiple_of(r * Q, Q), Q)

    @pl.when(s == 0)
    def _():
        d_hi, d_lo = split(dinv[0, own_quarter, :])
        out_ref[2 * CW :] = mm(r0, d_hi, d_lo, 1)

    @pl.when(s == 1)
    def _():
        d_hi, d_lo = split(dinv[1, own_quarter, :])
        out_ref[2 * CW :] = mm(t1, d_hi, d_lo, 1)

    @pl.when(x != 0)
    def _():
        red_copy.wait_send()

    for bytes_of, sem in (
        (of_redl, redl_s), (of_near, near_s), (of_far, far_s), (of_all, all_s), (of_row, fy_s), (of_row, fc_s), (of_rland, rl_s)
    ):
        departed(bytes_of, sem)
    for copy in x_copies + y_copies + xag_copies:
        copy.wait_send()
    for k in range(4):
        fwd_copy(0, k, h).wait_send()
        fwd_copy(1, k, h).wait_send()
    for k in range(4):
        xfwd_copy(k, h).wait_send()
    for copy in pair_p + pair_m + sum_p + sum_m:
        copy.wait_send()


def on_device(child_factor, child_map, child_len, class_ids, class_kappa, landmarks, diag_inverse):
    vmem = pl.BlockSpec(memory_space=pltpu.VMEM)
    hbm = pl.BlockSpec(memory_space=pltpu.HBM)
    dma = pltpu.SemaphoreType.DMA
    tile = (2 * CW, Q)
    out = pl.pallas_call(
        kernel,
        out_shape=pltpu.VMEM((2 * CW + NLAND, Q), F32),
        in_specs=[hbm] * 7,
        out_specs=vmem,
        scratch_shapes=[
            pltpu.VMEM((1, NROW * NODEQ), jnp.int32),
            pltpu.SMEM((1,), jnp.int32),
            pltpu.VMEM((64, Q), jnp.int32),
            pltpu.SMEM((8,), F32),
            pltpu.VMEM((1, 256), jnp.int32),
            pltpu.VMEM((KCH, NODEQ), F32),
            pltpu.VMEM((2, PW, PW), F32),
            pltpu.VMEM((KCH, NODEQ), BF16),
            pltpu.VMEM((KCH, NODEQ), BF16),
            pltpu.VMEM((2 * CW, KCH), F32),
            pltpu.VMEM((2 * CW, KCH), F32),
            pltpu.VMEM((NROW, NLAND, KCH), F32),
            pltpu.VMEM((4 * CW, NODEQ), BF16),
            pltpu.VMEM(tile, F32),
            pltpu.VMEM((NEAR, 2 * CW // NEAR, Q), F32),
            pltpu.VMEM((2 * CW // NEAR, Q), F32),
            pltpu.VMEM((NEAR, 2 * CW // NEAR, Q), F32),
            pltpu.VMEM((2 * CW // NEAR, Q), F32),
            pltpu.VMEM(tile, F32),
            pltpu.VMEM((2, 2, 4, NROW, CW // 2, Q), F32),
            pltpu.VMEM((NROW, 2 * NLAND, Q), F32),
            pltpu.VMEM((2, PW, PW), BF16),
            pltpu.VMEM((2, PW, PW), BF16),
            pltpu.VMEM((8, 2) + tile, F32),
            pltpu.VMEM((4,) + tile, F32),
            pltpu.VMEM((3,) + tile, F32),
            pltpu.VMEM((4,) + tile, F32),
            pltpu.VMEM((4,) + tile, F32),
            pltpu.VMEM((NCOL,) + tile, F32),
            dma((7,)), dma((1,)), dma((1,)), dma, dma,
            dma, dma, dma, dma, dma, dma,
            dma, dma, dma, dma, dma((2, 4)), dma((2, 4)), dma((2, 4)), dma((2, 4)), dma, dma,
            dma((4,)), dma((4,)), dma((3,)), dma((3,)), dma((4,)), dma((4,)), dma((4,)), dma((4,)),
            dma((4,)), dma((4,)), dma((4,)), dma((4,)),
        ],
        compiler_params=pltpu.CompilerParams(
            collective_id=0, has_side_effects=True, vmem_limit_bytes=63 << 20
        ),
    )(
        child_factor, child_map, child_len, class_ids.reshape(64, Q), class_kappa,
        landmarks.reshape(1, 256), diag_inverse,
    )
    return out[: 2 * CW].reshape(2, CW, 1, Q), out[2 * CW :].reshape(NLAND, 1, Q)


def solution(mesh):
    return jax.shard_map(
        on_device,
        mesh=mesh,
        in_specs=(P("sub", None, "row"), P("sub", None), P("sub"), P(), P(), P(), P()),
        out_specs=(P(None, "col", "sub", "row"), P("col", "sub", "row")),
        check_vma=False,
    )
```

```python
import jax
import jax.numpy as jnp
from jax import lax
from jax.experimental import pallas as pl
from jax.experimental.pallas import tpu as pltpu
from jax.sharding import PartitionSpec as P

F32 = jnp.float32
BF16 = jnp.bfloat16
MESH = pl.DeviceIdType.MESH

NSUB, NROW, NCOL = 16, 4, 8
NEAR = 4
ORDER = (1, 2, 3, 4, 5)
PW, Q, CW, KCH, NODEQ, NLAND = 512, 128, 64, 256, 512, 32


def dg(a, b, ca, cb):
    return lax.dot_general(a, b, (((ca,), (cb,)), ((), ())), preferred_element_type=F32)


def split(x):
    hi = x.astype(BF16)
    return hi, (x - hi.astype(F32)).astype(BF16)


def mm(a, b_hi, b_lo, cb):
    n = a.shape[0]
    a_hi, a_lo = split(a)
    both = dg(jnp.concatenate([a_hi, a_lo], axis=0), b_hi, 1, cb)
    return both[:n] + both[n:] + dg(a_hi, b_lo, 1, cb)


def mod(a, n):
    return lax.rem(a, jnp.int32(n))


def lanes(shape):
    return lax.broadcasted_iota(jnp.int32, shape, 1)


def rows_of(shape):
    return lax.broadcasted_iota(jnp.int32, shape, 0)


def kernel(
    factor_hbm, map_hbm, len_hbm, ids_hbm, kappa_hbm, land_hbm, dinv_hbm,
    out_ref,
    map_ref, len_ref, ids_ref, kappa_ref, land_ref, factor, dinv, live_hi, live_lo, red_out, red_in, redl, pst,
    top_out, near_in, near_sum, far_in, near_all, top_all, front_top, rland, s_hi, s_lo,
    terms, pre_p, pre_m, go_p, go_m, fx,
    ld_sem, red_s, red_r, redl_s, redl_r, near_s, near_r, far_s, far_r, all_s, all_r,
    fy_s, fy_r, fc_s, fc_r, fx_s, fx_r, fwd_s, fwd_r, rl_s, rl_r,
    pp_s, pp_r, pm_s, pm_r, gp_s, gp_r, gm_s, gm_r, xa_s, xa_r, xf_s, xf_r,
):
    s = lax.axis_index("sub")
    r = lax.axis_index("row")
    c = lax.axis_index("col")
    x, h = lax.div(c, 2), mod(c, 2)
    far, near = lax.div(s, NEAR), mod(s, NEAR)
    other = {"col": 2 * x + 1 - h}
    group = 2 * mod(r + x, NROW) + h
    right = {"sub": mod(s + 1, NSUB)}
    left = {"sub": mod(s + NSUB - 1, NSUB)}
    right2 = {"sub": mod(s + 2, NSUB)}
    left2 = {"sub": mod(s + NSUB - 2, NSUB)}

    def near_id(k):
        return {"sub": far * NEAR + mod(near + k, NEAR)}

    def far_id(k):
        return {"sub": mod(s + k * NEAR, NSUB)}

    def row_id(k):
        return {"row": mod(r + k, NROW)}

    def x_id(k):
        return {"col": 2 * mod(x + k, 4) + h}

    def remote(src, dst, send, recv, where):
        return pltpu.make_async_remote_copy(
            src_ref=src, dst_ref=dst, send_sem=send, recv_sem=recv, device_id=where, device_id_type=MESH
        )

    three = pl.ds(0, 3)
    of_redl, of_near, of_far = redl.at[three], near_in.at[three], far_in.at[three]
    of_all, of_row, of_rland = top_all.at[pl.ds(0, 3 * 2 * CW // NEAR)], front_top.at[0, 0, 0, three], rland.at[three]

    def arrived(bytes_of, sem):
        remote(bytes_of, bytes_of, sem, sem, other).wait_recv()

    def departed(bytes_of, sem):
        remote(bytes_of, bytes_of, sem, sem, other).wait_send()

    load_factor = pltpu.make_async_copy(factor_hbm.at[0], factor, ld_sem.at[0])
    load_factor.start()
    small = [
        pltpu.make_async_copy(src, dst, ld_sem.at[2 + k])
        for k, (src, dst) in enumerate(
            [(map_hbm, map_ref), (land_hbm, land_ref), (len_hbm, len_ref), (ids_hbm, ids_ref), (kappa_hbm, kappa_ref)]
        )
    ]
    for copy in small:
        copy.start()
    load_dinv = pltpu.make_async_copy(dinv_hbm, dinv, ld_sem.at[1])
    load_dinv.start()
    barrier = pltpu.get_barrier_semaphore()

    for peer in [right, left, right2, left2, other] + [make(k) for make in (near_id, far_id, row_id, x_id) for k in (1, 2, 3)]:
        pl.semaphore_signal(barrier, inc=1, device_id=peer, device_id_type=MESH)

    for copy in small:
        copy.wait()
    node_row = map_ref[:, pl.ds(pl.multiple_of(r * NODEQ, NODEQ), NODEQ)]
    land_row = land_ref[...]
    land_col = jnp.sum(
        jnp.where(lanes((NLAND, 256)) == rows_of((NLAND, 256)) + c * NLAND, land_row.astype(F32), 0.0),
        axis=1, keepdims=True,
    ).astype(jnp.int32)
    iota_col = rows_of((2 * CW, 1))
    send_cols = iota_col // CW * PW + (2 * r + h) * CW + iota_col % CW
    own_cols = iota_col // CW * PW + group * CW + iota_col % CW
    select = jnp.concatenate([send_cols, land_col], axis=0) == node_row
    select = jnp.where(select, 1.0, 0.0).astype(BF16)
    load_factor.wait()
    live = jnp.where(lanes((KCH, NODEQ)) + r * NODEQ < len_ref[0], factor[...], 0.0)
    lh, ll = split(live)
    live_hi[...] = lh
    live_lo[...] = ll
    reduced = dg(select, lh, 1, 1) + dg(select, ll, 1, 1)
    red_out[...] = reduced[: 2 * CW]
    redl[r] = reduced[2 * CW :]

    pl.semaphore_wait(barrier, 17)

    red_copy = remote(red_out, red_in, red_s.at[0], red_r.at[0], {"row": mod(r - x + NROW, NROW)})

    @pl.when(x != 0)
    def _():
        red_copy.start()

    @pl.when(x == 0)
    def _():
        red_in[...] = red_out[...]

    redl_copies = [remote(redl.at[r], redl.at[r], redl_s, redl_r, row_id(k)) for k in (1, 2, 3)]
    for copy in redl_copies:
        copy.start()

    def band(columns, block):
        index = block * NROW + r
        near = jnp.concatenate(
            [
                ids_ref[pl.ds(jnp.maximum(index - 1, 0), 1), :],
                ids_ref[pl.ds(index, 1), :],
                ids_ref[pl.ds(jnp.minimum(index + 1, 63), 1), :],
            ],
            axis=1,
        )
        coef = jnp.zeros(near.shape, F32)
        for k in range(8):
            coef = jnp.where(near == k, kappa_ref[k], coef)
        coef = coef + 4.0
        here = coef[:, Q : 2 * Q]
        before = pltpu.roll(coef, 1, 1)[:, Q : 2 * Q]
        after = pltpu.roll(coef, 3 * Q - 1, 1)[:, Q : 2 * Q]
        row = index * Q + lanes((1, Q))
        ends = jnp.where((row == 0) | (row == 64 * Q - 1), 1.0, 2.0)
        off = row - columns
        return jnp.where(
            off == 0, here * here + ends,
            jnp.where(
                off == 1, -(here + before),
                jnp.where(off == -1, -(here + after), jnp.where(jnp.abs(off) == 2, 1.0, 0.0)),
            ),
        )

    load_dinv.wait()
    for k in range(2):
        d_hi, d_lo = split(dinv[k])
        gram = dg(d_hi, d_hi, 0, 0) + dg(d_hi, d_lo, 0, 0) + dg(d_lo, d_hi, 0, 0)
        g_hi, g_lo = split(gram)
        s_hi[k] = g_hi
        s_lo[k] = g_lo

    target = node_row // PW * Q + node_row % Q
    top_band = jnp.concatenate(
        [band(own_cols[:CW], 1), band(land_col, 0), band(land_col, 1)], axis=0
    )
    top_band = jnp.where(s == 0, top_band, 0.0)
    own_band = band(own_cols, s)

    @pl.when(x != 0)
    def _():
        red_copy.wait_recv()

    arrived(of_redl, redl_r)
    reduced_all = jnp.concatenate([red_in[...], redl[0] + redl[1] + redl[2] + redl[3]], axis=0)
    part = -mm(reduced_all, live_hi[...], live_lo[...], 0)
    part_hi, part_lo = split(part)
    pst[...] = jnp.concatenate([part_hi[: 2 * CW], part_lo[: 2 * CW]], axis=0)

    def term(k):
        block_a, block_b = mod(s + 8 - k, NSUB), mod(s + 9 + k, NSUB)
        place = rows_of((2 * Q, 1))
        place = jnp.where(place < Q, block_a * Q + place, block_b * Q + place - Q)
        place = jnp.where(target == place, 1.0, 0.0).astype(BF16)
        both = dg(pst[...], place, 1, 1)
        both = both[: 2 * CW] + both[2 * CW :]
        terms[k, 0] = both[:, :Q]
        terms[k, 1] = both[:, Q:]

    pair_p = [remote(terms.at[2 * k, 0], pre_p.at[k], pp_s.at[k], pp_r.at[k], right) for k in range(4)]
    pair_m = [remote(terms.at[2 * k + 1, 1], pre_m.at[k], pm_s.at[k], pm_r.at[k], left) for k in range(3)]
    sum_p = [remote(pre_p.at[k], go_p.at[k], gp_s.at[k], gp_r.at[k], right2 if k < 3 else right) for k in range(4)]
    sum_m = [remote(terms.at[0, 1], go_m.at[0], gm_s.at[0], gm_r.at[0], left2)] + [
        remote(pre_m.at[k - 1], go_m.at[k], gm_s.at[k], gm_r.at[k], left2 if k < 3 else left) for k in (1, 2, 3)
    ]

    def pass_p(k):
        pair_p[k].wait_recv()
        if k == 0:
            pre_p[k] += terms[1, 0]
        else:
            sum_p[k - 1].wait_recv()
            pre_p[k] += go_p[k - 1] + terms[2 * k + 1, 0]
        sum_p[k].start()

    def pass_m(k):
        pair_m[k - 1].wait_recv()
        sum_m[k - 1].wait_recv()
        pre_m[k - 1] += go_m[k - 1] + terms[2 * k, 1]
        sum_m[k].start()

    place_top = jnp.where(target == rows_of((2 * Q, 1)), 1.0, 0.0).astype(BF16)
    top = dg(jnp.concatenate([part_hi, part_lo], axis=0), place_top, 1, 1)
    top = top[: 2 * CW + NLAND] + top[2 * CW + NLAND :]
    top_out[...] = top_band + jnp.concatenate(
        [top[:CW, Q:], top[2 * CW :, :Q], top[2 * CW :, Q:]], axis=0
    )

    near_rows = 2 * CW // NEAR

    def quarter_rows(k):
        return pl.ds(pl.multiple_of(k * near_rows, near_rows), near_rows)

    near_copies = [
        remote(top_out.at[quarter_rows(mod(near + k, NEAR))], near_in.at[near], near_s, near_r, near_id(k))
        for k in (1, 2, 3)
    ]
    for copy in near_copies:
        copy.start()
    near_in[near] = top_out[quarter_rows(near), :]

    term(0)
    pair_p[0].start()
    sum_m[0].start()
    term(1)
    pair_m[0].start()
    term(2)
    pair_p[1].start()

    far_copies = [remote(near_sum, far_in.at[far], far_s, far_r, far_id(k)) for k in (1, 2, 3)]
    all_copies = [remote(near_all, top_all.at[quarter_rows(near)], all_s, all_r, near_id(k)) for k in (1, 2, 3)]
    half = CW // 2
    row_copies = [
        remote(top_all.at[pl.ds(0, half)], front_top.at[h, 0, x, r], fy_s, fy_r, row_id(k)) for k in (1, 2, 3)
    ]
    col_copies = [
        remote(top_all.at[pl.ds(half, half)], front_top.at[h, 1, r, x], fc_s, fc_r, x_id(k)) for k in (1, 2, 3)
    ]
    rland_copies = [
        remote(top_all.at[pl.ds(CW, 2 * NLAND)], rland.at[r], rl_s, rl_r, row_id(k)) for k in (1, 2, 3)
    ]

    def wide_copy(part, src, dst, where):
        piece = front_top.at[h, part, src]
        return remote(piece, piece, fx_s.at[part, dst], fx_r.at[part, src], where)

    def fwd_copy(part, src, core):
        piece = front_top.at[core, part, src]
        return remote(piece, piece, fwd_s.at[part, src], fwd_r.at[part, src], other)

    x_copies = [wide_copy(0, x, mod(x + k, 4), x_id(k)) for k in (1, 2, 3)]
    y_copies = [wide_copy(1, r, mod(r + k, 4), row_id(k)) for k in (1, 2, 3)]

    def near_step():
        arrived(of_near, near_r)
        near_sum[...] = near_in[0] + near_in[1] + near_in[2] + near_in[3]
        for copy in far_copies:
            copy.start()
        far_in[far] = near_sum[...]

    def far_step():
        arrived(of_far, far_r)
        near_all[...] = far_in[0] + far_in[1] + far_in[2] + far_in[3]
        for copy in all_copies:
            copy.start()
        top_all[quarter_rows(near), :] = near_all[...]

    def all_step():
        arrived(of_all, all_r)
        for copy in row_copies + col_copies + rland_copies:
            copy.start()
        front_top[h, 0, x, r] = top_all[:half]
        front_top[h, 1, r, x] = top_all[half:CW]
        rland[r] = top_all[CW:]

    def row_step():
        arrived(of_row, fy_r)
        for copy in x_copies:
            copy.start()
        arrived(of_row, fc_r)
        for copy in y_copies:
            copy.start()
        fwd_copy(0, x, h).start()
        fwd_copy(1, r, h).start()

    def x_step():
        for k in (1, 3, 2):
            from_x, from_row = mod(x + k, 4), mod(r + k, 4)
            wide_copy(0, from_x, x, other).wait_recv()
            fwd_copy(0, from_x, h).start()
            wide_copy(1, from_row, r, other).wait_recv()
            fwd_copy(1, from_row, h).start()

    top_steps = (near_step, far_step, all_step, row_step, x_step)

    def tops(step):
        for top_step, place in zip(top_steps, ORDER):
            if place == step:
                top_step()

    for step in range(4):
        if step:
            pass_m(step)
        pass_p(step)
        tops(step + 1)
        if step < 2:
            term(2 * step + 3)
            pair_m[step + 1].start()
            term(2 * step + 4)
            pair_p[step + 2].start()
        if step == 2:
            term(7)

    own = terms[7, 1] + own_band
    sum_m[3].wait_recv()
    sum_p[3].wait_recv()
    fx[group] = own + go_m[3] + go_p[3]

    def slot(px, ph):
        return 2 * mod(r + px, NROW) + ph

    def xag_copy(src_x, dst_x, where):
        return remote(fx.at[slot(src_x, h)], fx.at[slot(src_x, h)], xa_s.at[dst_x], xa_r.at[src_x], where)

    def xfwd_copy(px, ph):
        return remote(fx.at[slot(px, ph)], fx.at[slot(px, ph)], xf_s.at[px], xf_r.at[px], other)

    xag_copies = [xag_copy(x, mod(x + k, 4), x_id(k)) for k in (1, 2, 3)]
    for copy in xag_copies:
        copy.start()
    xfwd_copy(x, h).start()

    tops(5)

    for k in range(4):
        fwd_copy(0, k, 1 - h).wait_recv()
        fwd_copy(1, k, 1 - h).wait_recv()
    arrived(of_rland, rl_r)
    f_hi, f_lo = split(
        jnp.concatenate(
            [
                jnp.concatenate(
                    [
                        piece
                        for g in range(NCOL)
                        for piece in (
                            front_top[g % 2, 0, (g // 2 - k) % 4, k], front_top[g % 2, 1, k, (g // 2 - k) % 4]
                        )
                    ],
                    axis=0,
                )
                for k in range(NROW)
            ],
            axis=1,
        )
    )
    r0 = jnp.concatenate([rland[k, :NLAND] for k in range(NROW)], axis=1)
    r1 = jnp.concatenate([rland[k, NLAND:] for k in range(NROW)], axis=1)
    own_rows = pl.ds(pl.multiple_of(c * CW, CW), CW)
    d0_own = dinv[0, own_rows, :]
    d1_own = dinv[1, own_rows, :]
    w0 = mm(r0, s_hi[0], s_lo[0], 0)
    t1 = r1 - mm(w0, f_hi, f_lo, 0)
    w1 = mm(t1, s_hi[1], s_lo[1], 0)
    back = mm(jnp.concatenate([d1_own, w1], axis=0), f_hi, f_lo, 1)
    back = mm(back, s_hi[0], s_lo[0], 0)
    column = lanes((NLAND, PW))
    e0 = jnp.where(column == land_col, 1.0, 0.0)
    e1 = jnp.where(column + PW == land_col, 1.0, 0.0)
    left0 = jnp.concatenate([d0_own, -back[:CW], e0 - w0 + back[CW:]], axis=0)
    left1 = jnp.concatenate([d1_own, e1 - w1], axis=0)

    for k in (1, 3, 2):
        from_x = mod(x + k, 4)
        xag_copy(from_x, x, other).wait_recv()
        xfwd_copy(from_x, h).start()
    for k in range(4):
        xfwd_copy(k, 1 - h).wait_recv()
    f0_hi, f0_lo = split(jnp.concatenate([fx[k, :CW] for k in range(NCOL)], axis=0))
    f1_hi, f1_lo = split(jnp.concatenate([fx[k, CW:] for k in range(NCOL)], axis=0))
    out0 = mm(left0, f0_hi, f0_lo, 0)
    out1 = mm(left1, f1_hi, f1_lo, 0)
    row_in = s * PW + r * Q + lanes((CW, Q))
    col_in = c * CW + rows_of((CW, Q))
    out_ref[:CW] = jnp.where(row_in >= col_in, out0[:CW], 0.0)
    out_ref[CW : 2 * CW] = jnp.where(row_in - PW >= col_in, out0[CW : 2 * CW] + out1[:CW], 0.0)
    out_ref[2 * CW :] = out0[2 * CW :] + out1[CW:]

    own_quarter = pl.ds(pl.multiple_of(r * Q, Q), Q)

    @pl.when(s == 0)
    def _():
        d_hi, d_lo = split(dinv[0, own_quarter, :])
        out_ref[2 * CW :] = mm(r0, d_hi, d_lo, 1)

    @pl.when(s == 1)
    def _():
        d_hi, d_lo = split(dinv[1, own_quarter, :])
        out_ref[2 * CW :] = mm(t1, d_hi, d_lo, 1)

    @pl.when(x != 0)
    def _():
        red_copy.wait_send()

    for bytes_of, sem in (
        (of_redl, redl_s), (of_near, near_s), (of_far, far_s), (of_all, all_s), (of_row, fy_s), (of_row, fc_s), (of_rland, rl_s)
    ):
        departed(bytes_of, sem)
    for copy in x_copies + y_copies + xag_copies:
        copy.wait_send()
    for k in range(4):
        fwd_copy(0, k, h).wait_send()
        fwd_copy(1, k, h).wait_send()
    for k in range(4):
        xfwd_copy(k, h).wait_send()
    for copy in pair_p + pair_m + sum_p + sum_m:
        copy.wait_send()


def on_device(child_factor, child_map, child_len, class_ids, class_kappa, landmarks, diag_inverse):
    vmem = pl.BlockSpec(memory_space=pltpu.VMEM)
    hbm = pl.BlockSpec(memory_space=pltpu.HBM)
    dma = pltpu.SemaphoreType.DMA
    tile = (2 * CW, Q)
    out = pl.pallas_call(
        kernel,
        out_shape=pltpu.VMEM((2 * CW + NLAND, Q), F32),
        in_specs=[hbm] * 7,
        out_specs=vmem,
        scratch_shapes=[
            pltpu.VMEM((1, NROW * NODEQ), jnp.int32),
            pltpu.SMEM((1,), jnp.int32),
            pltpu.VMEM((64, Q), jnp.int32),
            pltpu.SMEM((8,), F32),
            pltpu.VMEM((1, 256), jnp.int32),
            pltpu.VMEM((KCH, NODEQ), F32),
            pltpu.VMEM((2, PW, PW), F32),
            pltpu.VMEM((KCH, NODEQ), BF16),
            pltpu.VMEM((KCH, NODEQ), BF16),
            pltpu.VMEM((2 * CW, KCH), F32),
            pltpu.VMEM((2 * CW, KCH), F32),
            pltpu.VMEM((NROW, NLAND, KCH), F32),
            pltpu.VMEM((4 * CW, NODEQ), BF16),
            pltpu.VMEM(tile, F32),
            pltpu.VMEM((NEAR, 2 * CW // NEAR, Q), F32),
            pltpu.VMEM((2 * CW // NEAR, Q), F32),
            pltpu.VMEM((NEAR, 2 * CW // NEAR, Q), F32),
            pltpu.VMEM((2 * CW // NEAR, Q), F32),
            pltpu.VMEM(tile, F32),
            pltpu.VMEM((2, 2, 4, NROW, CW // 2, Q), F32),
            pltpu.VMEM((NROW, 2 * NLAND, Q), F32),
            pltpu.VMEM((2, PW, PW), BF16),
            pltpu.VMEM((2, PW, PW), BF16),
            pltpu.VMEM((8, 2) + tile, F32),
            pltpu.VMEM((4,) + tile, F32),
            pltpu.VMEM((3,) + tile, F32),
            pltpu.VMEM((4,) + tile, F32),
            pltpu.VMEM((4,) + tile, F32),
            pltpu.VMEM((NCOL,) + tile, F32),
            dma((7,)), dma((1,)), dma((1,)), dma, dma,
            dma, dma, dma, dma, dma, dma,
            dma, dma, dma, dma, dma((2, 4)), dma((2, 4)), dma((2, 4)), dma((2, 4)), dma, dma,
            dma((4,)), dma((4,)), dma((3,)), dma((3,)), dma((4,)), dma((4,)), dma((4,)), dma((4,)),
            dma((4,)), dma((4,)), dma((4,)), dma((4,)),
        ],
        compiler_params=pltpu.CompilerParams(
            collective_id=0, has_side_effects=True, vmem_limit_bytes=63 << 20
        ),
    )(
        child_factor, child_map, child_len, class_ids.reshape(64, Q), class_kappa,
        landmarks.reshape(1, 256), diag_inverse,
    )
    return out[: 2 * CW].reshape(2, CW, 1, Q), out[2 * CW :].reshape(NLAND, 1, Q)


def solution(mesh):
    return jax.shard_map(
        on_device,
        mesh=mesh,
        in_specs=(P("sub", None, "row"), P("sub", None), P("sub"), P(), P(), P(), P()),
        out_specs=(P(None, "col", "sub", "row"), P("col", "sub", "row")),
        check_vma=False,
    )
```
